256 devices in a mesh: ctx: 16 (over x_hi, y, core), head: 16 (over x_lo, z).
Axes of the slice: x: 4 (x_hi: 2, x_lo: 2; x = x_hi * 2 + x_lo), y: 4, z: 8, core: 2. Of those that a mesh axis runs over, the one named last changes fastest.
Arguments:
- new_states: bfloat16 [2048, 8192], P('ctx', 'head'), may hold values from -6 to 6
- query_weight: bfloat16 [8192, 8192], P(None, 'head'), may hold values from -0.0625 to 0.0625
- key_weight: bfloat16 [8192, 1024], P(None, 'head'), may hold values from -0.0625 to 0.0625
- value_weight: bfloat16 [8192, 1024], P(None, 'head'), may hold values from -0.0625 to 0.0625
- cache_keys: bfloat16 [18432, 1024], P('ctx', 'head'), may hold values from -480 to 480
- cache_values: bfloat16 [18432, 1024], P('ctx', 'head'), may hold values from -6 to 6
- new_positions: int32 [2048], P('ctx'), may hold values from 18432 to 20479, as said below
Outputs:
- attended: bfloat16 [2048, 8192], P('ctx', 'head')
The draws below stay inside these ranges and needn't reach their ends.
Inputs may be any that keep to these rules, and one draw needn't show every extreme that they name: `new_positions`: the appended rows hold each position from 18432 to 20479 once, in runs of 8 consecutive positions.
All inputs are finite; a program needn't handle non-finite values.
Results may differ from the reference program's by a relative error of at most 0.04.
Values may be sent and summed in bfloat16 or wider, within the bound.
A program may use at most 128 MiB of HBM per device.

```python
import math
import jax
import jax.numpy as jnp
from jax import lax

D = 8192
HD = 128
GROUP = 8
RUN = 8
QHEADS = 64
KVH = 8
CACHED = 18432
NEW_ROWS = 2048


def draw_new_positions(key, part):
    run_count = NEW_ROWS // RUN
    order = jax.random.permutation(key, run_count).astype(jnp.int32)
    offsets = order[:, None] * RUN + jnp.arange(RUN, dtype=jnp.int32)[None, :]
    return (CACHED + offsets.reshape(-1)).astype(jnp.int32)


def draw_cache_keys(key, part):
    base = jax.random.normal(key, (CACHED, KVH * HD), jnp.float32)
    base = jnp.clip(base, -6.0, 6.0)
    return base.astype(jnp.bfloat16)


def steps_of(stream_key, shape, cuts, low, largest):
    factor_of = 1.0
    for position, shards_of in cuts:
        draws = jax.random.uniform(jax.random.fold_in(jax.random.fold_in(stream_key, 6), position), (shards_of,), jnp.float32, low / len(cuts), largest / len(cuts))
        factor_of = factor_of * jnp.repeat(jnp.exp(draws), shape[position] // shards_of).reshape((-1,) + (1,) * (len(shape) - 1 - position))
    return factor_of


def noise(key, dims, deviation, reach, shards=(), kind=jnp.bfloat16):
    loudness = steps_of(key, dims, shards, -0.22, 0.18) if shards else 1.0
    drawn = jax.random.normal(key, dims, jnp.float32) * deviation * loudness
    return jnp.minimum(jnp.maximum(drawn, -reach), reach).astype(kind)


def setup_inputs(seed: int = 0) -> dict:
    keys = jax.random.split(jax.random.key(seed), 8)
    new_states = noise(keys[0], (NEW_ROWS, D), 1.0, 6.0, ((0, 16), (1, 16)))
    query_weight = noise(keys[1], (D, QHEADS * HD), D ** -0.5, 0.0625, ((1, 16),))
    key_weight = noise(keys[2], (D, KVH * HD), D ** -0.5, 0.0625, ((1, 16),))
    value_weight = noise(keys[3], (D, KVH * HD), D ** -0.5, 0.0625, ((1, 16),))
    cache_keys = draw_cache_keys(jax.random.fold_in(keys[7], 71), 0)
    cache_values = noise(keys[5], (CACHED, KVH * HD), 1.0, 6.0, ((0, 16), (1, 16)))
    new_positions = draw_new_positions(jax.random.fold_in(keys[7], 71), 0)
    return {"new_states": new_states, "query_weight": query_weight, "key_weight": key_weight, "value_weight": value_weight, "cache_keys": cache_keys, "cache_values": cache_values, "new_positions": new_positions}


THETA = 500000.0
NEGATIVE = -1e30


def rotary(values, positions):
    half_width = values.shape[-1] // 2
    freq_index = jnp.arange(half_width, dtype=jnp.float32)
    inverse = jnp.exp(freq_index * (-2.0 * math.log(THETA) / values.shape[-1]))
    angles = positions.astype(jnp.float32)[:, None] * inverse[None, :]
    cosine = jnp.cos(angles)[:, None, :]
    sine_part = jnp.sin(angles)[:, None, :]
    lower_part = values[..., :half_width]
    upper_part = values[..., half_width:]
    return jnp.concatenate([lower_part * cosine - upper_part * sine_part, upper_part * cosine + lower_part * sine_part], axis=-1)


def reference(new_states, query_weight, key_weight, value_weight, cache_keys, cache_values, new_positions):
    positions = new_positions.astype(jnp.int32)
    queries = jnp.dot(new_states, query_weight, preferred_element_type=jnp.float32).reshape(NEW_ROWS, QHEADS, HD)
    queries = (rotary(queries, positions) * (HD ** -0.5)).astype(jnp.bfloat16)
    raw_keys = jnp.dot(new_states, key_weight, preferred_element_type=jnp.float32).astype(jnp.bfloat16)
    new_keys = rotary(raw_keys.astype(jnp.float32).reshape(NEW_ROWS, KVH, HD), positions).astype(jnp.bfloat16)
    new_values = jnp.dot(new_states, value_weight, preferred_element_type=jnp.float32).astype(jnp.bfloat16)
    all_keys = jnp.concatenate([cache_keys.reshape(CACHED, KVH, HD), new_keys], axis=0).transpose(1, 0, 2)
    all_values = jnp.concatenate([cache_values.reshape(CACHED, KVH, HD), new_values.reshape(NEW_ROWS, KVH, HD)], axis=0).transpose(1, 0, 2)
    key_positions = jnp.concatenate([jnp.zeros((CACHED,), jnp.int32), positions])
    visible = key_positions[None, :] <= positions[:, None]

    def one_head(head_index):
        kv_group = head_index // GROUP
        keys_here = all_keys[kv_group]
        values_here = all_values[kv_group]
        query_here = queries[:, head_index, :]
        scores = jnp.dot(query_here, keys_here.T, preferred_element_type=jnp.float32)
        scores = jnp.where(visible, scores, NEGATIVE)
        highest = jnp.max(scores, axis=1, keepdims=True)
        weights = jnp.where(visible, jnp.exp(scores - highest), 0.0)
        weight_sum = jnp.sum(weights, axis=1, keepdims=True)
        mixed_sum = jnp.dot(weights.astype(jnp.bfloat16), values_here, preferred_element_type=jnp.float32)
        return (mixed_sum / weight_sum).astype(jnp.bfloat16)

    outputs = lax.map(one_head, jnp.arange(QHEADS, dtype=jnp.int32))
    return outputs.transpose(1, 0, 2).reshape(NEW_ROWS, QHEADS * HD)
```

```python
import math

import jax
import jax.numpy as jnp
from jax import lax
from jax.experimental import pallas as pl
from jax.experimental.pallas import tpu as pltpu
from jax.sharding import PartitionSpec as P

THETA = 500000.0
NEGATIVE = -1e30
MESH = pl.DeviceIdType.MESH
LOG2E = math.log2(math.e)

ROWS = 128
COLS = 512
HEAD = 128
HALF = 64
CACHE = 1152
QROWS = 512
SLOTS = 8
CUT = 128
SENDS = 64
NT = (((1,), (1,)), ((), ()))


def kernel(
    x_hbm, wq_hbm, wk_hbm, wv_hbm, ck_hbm, cv_hbm, pos_row, pos_col, cos_q, sin_q, cos_k, sin_k,
    out_ref,
    xbuf, wq, wkv, kvc, kvn, raw, qs, pos_far, q_sum, kv_sum, top, total, acc, o_out, o_in, st_out, st_in,
    local_sem, x_sem, kv_sem, kvn_sem, one_sem, send_sem,
):
    c = lax.axis_index("ctx")
    h = lax.axis_index("head")
    xh, yy, pp = c // 8, (c // 2) % 4, c % 2
    xl, z = h // 8, h % 8
    bit = h % 2
    away = 1 - bit

    def head_at(col, row):
        return col * 8 + (row + 8) % 8

    def ctx_at(row, core):
        return xh * 8 + ((row + 4) % 4) * 2 + core

    def slot_at(row, core):
        return ((row + 4) % 4) * 2 + core

    zp, zm = (c, head_at(xl, z + 1)), (c, head_at(xl, z - 1))
    xp = (c, head_at(1 - xl, z))
    pair = (c, h + 1 - 2 * bit)
    yp, ym = (ctx_at(yy + 1, pp), h), (ctx_at(yy - 1, pp), h)
    sib = (ctx_at(yy, 1 - pp), h)
    far = ((c + 8) % 16, h)
    mine = slot_at(yy, pp)

    pending = []

    def remote(src, dst, sem, device):
        copy = pltpu.make_async_remote_copy(
            src_ref=src, dst_ref=dst, send_sem=send_sem.at[len(pending)], recv_sem=sem,
            device_id=device, device_id_type=MESH,
        )
        pending.append(copy)
        copy.start()

    def arrived(ref, sem):
        pltpu.make_async_remote_copy(
            src_ref=ref, dst_ref=ref, send_sem=send_sem.at[0], recv_sem=sem,
            device_id=sib, device_id_type=MESH,
        ).wait_recv()

    def local(i, src, dst):
        copy = pltpu.make_async_copy(src, dst, local_sem.at[i])
        copy.start()
        return copy

    x_in = local(0, x_hbm, xbuf.at[h])
    k_in = local(1, ck_hbm, kvc.at[mine, bit, 0:HALF, :])
    v_in = local(2, cv_hbm, kvc.at[mine, bit, HALF:HEAD, :])
    wk_in = local(3, wk_hbm, wkv.at[0:HALF, :])
    wv_in = local(4, wv_hbm, wkv.at[HALF:HEAD, :])
    wq_in = [
        local(5 + i, wq_hbm.at[2048 * i : 2048 * (i + 1), :], wq.at[2048 * i : 2048 * (i + 1), :])
        for i in range(4)
    ]

    barrier = pltpu.get_barrier_semaphore()
    for device in (zp, zm, xp, yp, ym, sib, far):
        pl.semaphore_signal(barrier, inc=1, device_id=device, device_id_type=MESH)
    pl.semaphore_wait(barrier, 7)

    def piece(kind, slot):
        if kind == 0:
            return xbuf.at[slot, :, 0:CUT]
        return xbuf.at[slot, :, CUT:COLS]

    def send_x(kind, slot, device):
        remote(piece(kind, slot), piece(kind, slot), x_sem.at[kind, slot], device)

    def wait_x(kind, slot):
        arrived(piece(kind, slot), x_sem.at[kind, slot])

    def send_kv(slot, half, device):
        remote(kvc.at[slot, half], kvc.at[slot, half], kv_sem.at[slot, half], device)

    def wait_kv(slot, half):
        arrived(kvc.at[slot, half], kv_sem.at[slot, half])

    def send_new(slot, device):
        remote(kvn.at[slot], kvn.at[slot], kvn_sem.at[slot], device)

    def wait_new(slot):
        arrived(kvn.at[slot], kvn_sem.at[slot])

    x_in.wait()
    send_x(0, h, xp)
    for kind in (0, 1):
        send_x(kind, h, zp)
        send_x(kind, h, zm)
    send_x(1, h, xp)
    k_in.wait()
    v_in.wait()
    send_kv(mine, bit, pair)
    for device in (yp, ym, sib):
        send_kv(mine, bit, device)
    remote(pos_col, pos_far, one_sem.at[0], far)

    q_sum[...] = jnp.zeros_like(q_sum)
    kv_sum[...] = jnp.zeros_like(kv_sum)

    def project(slot):
        block = xbuf[slot]
        start = pl.multiple_of(slot * COLS, COLS)
        q_sum[...] += jnp.dot(block, wq[pl.ds(start, COLS), :], preferred_element_type=jnp.float32)
        kv_sum[...] += lax.dot_general(
            wkv[:, pl.ds(start, COLS)], block, NT, preferred_element_type=jnp.float32
        )

    reach = {(0, 1): 4, (0, -1): 3, (1, 1): 3, (1, -1): 4}

    def ring_step(t):
        for kind in (1, 0):
            for sign, ahead in ((1, zp), (-1, zm)):
                last = reach[kind, sign]
                if t > last:
                    continue
                slot = head_at(xl, z - sign * t)
                wait_x(kind, slot)
                if t < last:
                    send_x(kind, slot, ahead)
                if kind == 1:
                    send_x(1, slot, xp)
        if t == 1:
            slot = head_at(1 - xl, z)
            wait_x(0, slot)
            send_x(0, slot, zp)
            send_x(0, slot, zm)
        else:
            other_column(t - 1)

    def other_column(t):
        for sign, ahead in ((1, zp), (-1, zm)):
            last = reach[0, sign]
            if t > last:
                continue
            slot = head_at(1 - xl, z - sign * t)
            wait_x(0, slot)
            if t < last:
                send_x(0, slot, ahead)

    def other_rest(t):
        steps = (0,) if t == 0 else ((4,) if t == 4 else (t, -t))
        for step in steps:
            slot = head_at(1 - xl, z - step)
            wait_x(1, slot)
            project(slot)

    def own_column(t):
        steps = (0,) if t == 0 else ((4,) if t == 4 else (t, -t))
        for step in steps:
            project(head_at(xl, z - step))

    def kv_own_halves():
        wait_kv(mine, away)
        for device in (yp, ym, sib):
            send_kv(mine, away, device)

    def kv_from_sides(half):
        up, down = slot_at(yy - 1, pp), slot_at(yy + 1, pp)
        wait_kv(up, half)
        wait_kv(down, half)
        send_kv(slot_at(yy - 1 + 2 * half, pp), half, (ctx_at(yy + 1 - 2 * half, pp), h))
        send_kv(up, half, sib)
        send_kv(down, half, sib)

    ring_step(1)
    wk_in.wait()
    wv_in.wait()
    for copy in wq_in:
        copy.wait()
    own_column(0)
    ring_step(2)
    other_rest(0)
    own_column(1)
    kv_from_sides(bit)
    kv_own_halves()
    ring_step(3)
    other_rest(1)
    own_column(2)
    ring_step(4)
    other_column(4)
    other_rest(2)
    own_column(3)
    own_column(4)
    other_rest(3)
    other_rest(4)

    raw[bit] = kv_sum[...].astype(jnp.bfloat16)
    remote(raw.at[bit], raw.at[bit], one_sem.at[1], pair)
    cosine, sine = cos_q[...], sin_q[...]
    scale = HEAD**-0.5 * LOG2E
    for j in range(4):
        part = q_sum[:, HEAD * j : HEAD * (j + 1)]
        turned = part * cosine + pltpu.roll(part, HALF, 1) * sine
        qs[0, ROWS * j : ROWS * (j + 1), :] = (turned * scale).astype(jnp.bfloat16)
    remote(qs.at[0], qs.at[1], one_sem.at[2], far)

    arrived(raw.at[away], one_sem.at[1])
    lower, upper = raw[0].astype(jnp.float32), raw[1].astype(jnp.float32)
    low, high = lower[0:HALF], upper[0:HALF]
    cosine, sine = cos_k[...], sin_k[...]
    kvn[mine, 0:HALF, :] = (low * cosine - high * sine).astype(jnp.bfloat16)
    kvn[mine, HALF:HEAD, :] = (high * cosine + low * sine).astype(jnp.bfloat16)
    kvn[mine, HEAD : HEAD + HALF, :] = raw[0, HALF:HEAD, :]
    kvn[mine, HEAD + HALF : 2 * HEAD, :] = raw[1, HALF:HEAD, :]
    kvn[mine, 2 * HEAD :, :] = pos_row[...]
    for device in (yp, ym, sib):
        send_new(mine, device)

    top[...] = jnp.full_like(top, NEGATIVE)
    total[...] = jnp.zeros_like(total)
    acc[...] = jnp.zeros_like(acc)

    def attend(which, keys, values, hidden):
        scores = jnp.dot(qs[which], keys, preferred_element_type=jnp.float32)
        if hidden is not None:
            scores = jnp.where(hidden, NEGATIVE, scores)
        before = top[which, :, 0:1]
        now = jnp.maximum(before, jnp.max(scores, axis=1, keepdims=True))
        weights = jnp.exp2(scores - now)
        factor = jnp.exp2(before - now)
        total[which] = total[which] * factor + jnp.sum(weights, axis=1, keepdims=True)
        acc[which] = acc[which] * factor + lax.dot_general(
            weights.astype(jnp.bfloat16), values, NT, preferred_element_type=jnp.float32
        )
        top[which] = jnp.broadcast_to(now, (QROWS, HEAD))

    def attend_cached(which, slot):
        keys = jnp.concatenate([kvc[slot, 0, 0:HALF, :], kvc[slot, 1, 0:HALF, :]], axis=0)
        values = jnp.concatenate([kvc[slot, 0, HALF:HEAD, :], kvc[slot, 1, HALF:HEAD, :]], axis=0)
        attend(which, keys, values, None)

    def attend_new(which, where_ref):
        keys = jnp.concatenate([kvn[s, 0:HEAD, :] for s in range(SLOTS)], axis=1)
        values = jnp.concatenate([kvn[s, HEAD : 2 * HEAD, :] for s in range(SLOTS)], axis=1)
        code = jnp.concatenate([kvn[s, 2 * HEAD :, :] for s in range(SLOTS)], axis=1).astype(jnp.float32)
        key_pos = code[0:1] * 256.0 + code[1:2]
        code = where_ref[...].astype(jnp.float32)
        query_pos = code[:, 0:1] * 256.0 + code[:, 1:2]
        query_pos = jnp.concatenate([query_pos] * 4, axis=0)
        attend(which, keys, values, key_pos > query_pos)

    attend_cached(0, mine)
    kv_from_sides(away)
    wait_new(slot_at(yy - 1, pp))
    send_new(slot_at(yy - 1, pp), yp)
    send_new(slot_at(yy - 1, pp), sib)
    wait_new(slot_at(yy + 1, pp))
    send_new(slot_at(yy + 1, pp), sib)
    for core in (pp, 1 - pp):
        for row in (-1, 1):
            slot = slot_at(yy + row, core)
            if core is not pp:
                wait_kv(slot, 0)
                wait_kv(slot, 1)
            attend_cached(0, slot)
    opposite = slot_at(yy + 2, pp)
    wait_kv(opposite, 0)
    send_kv(opposite, 0, sib)
    wait_kv(opposite, 1)
    send_kv(opposite, 1, sib)
    wait_new(opposite)
    send_new(opposite, sib)
    wait_kv(slot_at(yy, 1 - pp), 0)
    wait_kv(slot_at(yy, 1 - pp), 1)
    attend_cached(0, slot_at(yy, 1 - pp))
    attend_cached(0, opposite)
    wait_kv(slot_at(yy + 2, 1 - pp), 0)
    wait_kv(slot_at(yy + 2, 1 - pp), 1)
    attend_cached(0, slot_at(yy + 2, 1 - pp))
    arrived(qs.at[1], one_sem.at[2])

    @pl.loop(0, SLOTS)
    def _(slot):
        attend_cached(1, slot)

    arrived(pos_far, one_sem.at[0])
    for row in (0, -1, 1, 2):
        wait_new(slot_at(yy + row, 1 - pp))
    attend_new(1, pos_far)
    o_out[...] = acc[1].astype(jnp.bfloat16)
    lane = lax.broadcasted_iota(jnp.int32, (ROWS, HEAD), 1)
    state = jnp.zeros((ROWS, HEAD), jnp.float32)
    for j in range(4):
        state = jnp.where(lane == j, top[1, ROWS * j : ROWS * (j + 1), :], state)
        state = jnp.where(lane == 4 + j, total[1, ROWS * j : ROWS * (j + 1), :], state)
    st_out[...] = state
    remote(st_out, st_in, one_sem.at[3], far)
    remote(o_out, o_in, one_sem.at[4], far)
    attend_new(0, pos_col)
    arrived(st_in, one_sem.at[3])
    arrived(o_in, one_sem.at[4])
    state = st_in[...]
    for j in range(4):
        rows = slice(ROWS * j, ROWS * (j + 1))
        here, there = top[0, rows, 0:1], state[:, j : j + 1]
        both = jnp.maximum(here, there)
        near_part, far_part = jnp.exp2(here - both), jnp.exp2(there - both)
        weight_sum = total[0, rows, 0:1] * near_part + state[:, 4 + j : 5 + j] * far_part
        mixed = acc[0, rows, :] * near_part + o_in[rows, :].astype(jnp.float32) * far_part
        out_ref[:, HEAD * j : HEAD * (j + 1)] = (mixed / weight_sum).astype(jnp.bfloat16)

    for copy in pending:
        copy.wait_send()


def per_device(
    new_states, query_weight, key_weight, value_weight, cache_keys, cache_values, new_positions
):
    inverse = jnp.exp(jnp.arange(HALF, dtype=jnp.float32) * (-2.0 * math.log(THETA) / HEAD))
    places = new_positions.astype(jnp.float32)
    angles = places[:, None] * inverse[None, :]
    cosine, sine = jnp.cos(angles), jnp.sin(angles)
    cos_q = jnp.concatenate([cosine, cosine], axis=1)
    sin_q = jnp.concatenate([-sine, sine], axis=1)
    turned = inverse[:, None] * places[None, :]
    cos_k, sin_k = jnp.cos(turned), jnp.sin(turned)
    coarse = (new_positions // 256).astype(jnp.bfloat16)
    fine = (new_positions % 256).astype(jnp.bfloat16)
    line = jnp.arange(16)[:, None]
    pos_row = jnp.where(line == 0, coarse[None, :], jnp.where(line == 1, fine[None, :], 0))
    line = jnp.arange(HEAD)[None, :]
    pos_col = jnp.where(line == 0, coarse[:, None], jnp.where(line == 1, fine[:, None], 0))

    hbm = pl.BlockSpec(memory_space=pl.ANY)
    vmem = pl.BlockSpec(memory_space=pltpu.VMEM)
    dma = pltpu.SemaphoreType.DMA
    bf16, f32 = jnp.bfloat16, jnp.float32
    return pl.pallas_call(
        kernel,
        out_shape=jax.ShapeDtypeStruct((ROWS, COLS), bf16),
        in_specs=[hbm] * 6 + [vmem] * 6,
        out_specs=vmem,
        scratch_shapes=[
            pltpu.VMEM((16, ROWS, COLS), bf16),
            pltpu.VMEM((8192, COLS), bf16),
            pltpu.VMEM((HEAD, 8192), bf16),
            pltpu.VMEM((SLOTS, 2, HEAD, CACHE), bf16),
            pltpu.VMEM((SLOTS, 2 * HEAD + 16, ROWS), bf16),
            pltpu.VMEM((2, HEAD, ROWS), bf16),
            pltpu.VMEM((2, QROWS, HEAD), bf16),
            pltpu.VMEM((ROWS, HEAD), bf16),
            pltpu.VMEM((ROWS, COLS), f32),
            pltpu.VMEM((HEAD, ROWS), f32),
            pltpu.VMEM((2, QROWS, HEAD), f32),
            pltpu.VMEM((2, QROWS, HEAD), f32),
            pltpu.VMEM((2, QROWS, HEAD), f32),
            pltpu.VMEM((QROWS, HEAD), bf16),
            pltpu.VMEM((QROWS, HEAD), bf16),
            pltpu.VMEM((ROWS, HEAD), f32),
            pltpu.VMEM((ROWS, HEAD), f32),
            dma((9,)),
            dma((2, 16)),
            dma((SLOTS, 2)),
            dma((SLOTS,)),
            dma((5,)),
            dma((SENDS,)),
        ],
        compiler_params=pltpu.CompilerParams(
            collective_id=0, has_side_effects=True, vmem_limit_bytes=56 << 20
        ),
    )(
        new_states, query_weight, key_weight.T, value_weight.T, cache_keys.T, cache_values.T,
        pos_row.astype(bf16), pos_col.astype(bf16), cos_q, sin_q, cos_k, sin_k,
    )


def solution(mesh):
    placed = (
        P("ctx", "head"),
        P(None, "head"),
        P(None, "head"),
        P(None, "head"),
        P("ctx", "head"),
        P("ctx", "head"),
        P("ctx"),
    )
    return jax.shard_map(
        per_device, mesh=mesh, in_specs=placed, out_specs=P("ctx", "head"), check_vma=False
    )
```

```python
import math

import jax
import jax.numpy as jnp
import numpy as np
from jax import lax
from jax.experimental import pallas as pl
from jax.experimental.pallas import tpu as pltpu
from jax.sharding import PartitionSpec as P

THETA = 500000.0
NEGATIVE = -1e30
MESH = pl.DeviceIdType.MESH
LOG2E = math.log2(math.e)

ROWS = 128
COLS = 512
HEAD = 128
HALF = 64
CACHE = 1152
QROWS = 512
PART = 256
LINES = 4
SENDS = 96
CUTS = ((0, 128), (128, 384), (384, 512))
REACH = {(0, 1): 4, (0, -1): 3, (1, 1): 3, (1, -1): 4, (2, 1): 4, (2, -1): 3}
NT = (((1,), (1,)), ((), ()))


def kernel(
    x_hbm, wq_hbm, wk_hbm, wv_hbm, ck_hbm, cv_hbm, pos_ref, turn_ref,
    out_ref,
    xbuf, wq, wkv, kvc, kvn, raw, qs, places, q_sum, kv_sum, top, total, acc, sbuf, nbuf,
    cos_q, sin_q, cos_k, sin_k, query_pos, o_out, o_in, st_out, st_in,
    local_sem, x_sem, kv_sem, kvn_sem, one_sem, send_sem,
):
    c = lax.axis_index("ctx")
    h = lax.axis_index("head")
    xh, yy, pp = c // 8, (c // 2) % 4, c % 2
    xl, z = h // 8, h % 8
    bit = h % 2
    away = 1 - bit
    other = 1 - pp

    def head_at(col, row):
        return col * 8 + (row + 8) % 8

    def ctx_at(row, core):
        return xh * 8 + ((row + 4) % 4) * 2 + core

    def line(step):
        return (yy + step + 4) % 4

    zp, zm = (c, head_at(xl, z + 1)), (c, head_at(xl, z - 1))
    xp = (c, head_at(1 - xl, z))
    pair = (c, h + 1 - 2 * bit)
    yp, ym = (ctx_at(yy + 1, pp), h), (ctx_at(yy - 1, pp), h)
    sib = (ctx_at(yy, other), h)
    far = ((c + 8) % 16, h)

    pending = []

    def remote(src, dst, sem, device, like=None):
        number = len(pending)
        pltpu.make_async_remote_copy(
            src_ref=src, dst_ref=dst, send_sem=send_sem.at[number], recv_sem=sem,
            device_id=device, device_id_type=MESH,
        ).start()
        pending.append(like or (lambda: src))

    def arrived(ref, sem):
        pltpu.make_async_remote_copy(
            src_ref=ref, dst_ref=ref, send_sem=send_sem.at[0], recv_sem=sem,
            device_id=sib, device_id_type=MESH,
        ).wait_recv()

    def local(i, src, dst):
        copy = pltpu.make_async_copy(src, dst, local_sem.at[i])
        copy.start()
        return copy

    def cached(row, half, core):
        return kvc.at[row, half, :, pl.ds(pl.multiple_of(core * CACHE, 128), CACHE)]

    own = pl.ds(pl.multiple_of(pp * CACHE, 128), CACHE)
    x_in = local(0, x_hbm, xbuf.at[h])
    k_in = local(1, ck_hbm, kvc.at[yy, bit, 0:HALF, own])
    v_in = local(2, cv_hbm, kvc.at[yy, bit, HALF:HEAD, own])
    wk_in = local(3, wk_hbm, wkv.at[0:HALF, :])
    wv_in = local(4, wv_hbm, wkv.at[HALF:HEAD, :])
    wq_in = [
        local(5 + i, wq_hbm.at[2048 * i : 2048 * (i + 1), :], wq.at[2048 * i : 2048 * (i + 1), :])
        for i in range(4)
    ]

    barrier = pltpu.get_barrier_semaphore()
    for device in (zp, zm, xp, yp, ym, sib, far):
        pl.semaphore_signal(barrier, inc=1, device_id=device, device_id_type=MESH)

    position = pos_ref[...]
    row_index = lax.broadcasted_iota(jnp.int32, (16, ROWS), 0)
    coarse = jnp.broadcast_to((position // 256).astype(jnp.float32), (16, ROWS))
    fine = jnp.broadcast_to((position % 256).astype(jnp.float32), (16, ROWS))
    places[0] = jnp.where(row_index == 0, coarse, jnp.where(row_index == 1, fine, 0.0)).astype(jnp.bfloat16)
    kvn[yy * 2 + pp, 2 * HEAD :, :] = places[0]
    pl.semaphore_wait(barrier, 7)

    def piece(kind, slot):
        return xbuf.at[slot, :, CUTS[kind][0] : CUTS[kind][1]]

    def send_x(kind, slot, device):
        remote(piece(kind, slot), piece(kind, slot), x_sem.at[kind, slot], device)

    def wait_x(kind, slot):
        arrived(piece(kind, slot), x_sem.at[kind, slot])

    def send_kv(row, half, core, device):
        block = cached(row, half, core)
        remote(block, block, kv_sem.at[row, half, core], device, lambda: kvc.at[0, 0, :, 0:CACHE])

    def wait_kv(row, half, core):
        arrived(cached(row, half, core), kv_sem.at[row, half, core])

    def send_new(row, core, device):
        slot = row * 2 + core
        remote(kvn.at[slot], kvn.at[slot], kvn_sem.at[slot], device, lambda: kvn.at[0])

    def wait_new(row, core):
        slot = row * 2 + core
        arrived(kvn.at[slot], kvn_sem.at[slot])

    across = head_at(1 - xl, z)

    def first_wave():
        x_in.wait()
        send_x(0, h, xp)
        for kind in (1, 0):
            send_x(kind, h, zp)
            send_x(kind, h, zm)
        send_x(1, h, xp)

    def second_wave():
        send_x(2, h, zp)
        send_x(2, h, zm)
        send_x(2, h, xp)
        wait_x(0, across)
        send_x(0, across, zp)
        send_x(0, across, zm)

    def ring(t, kind, col):
        for sign, ahead in ((1, zp), (-1, zm)):
            last = REACH[kind, sign]
            if t > last:
                continue
            slot = head_at(col, z - sign * t)
            wait_x(kind, slot)
            if t < last:
                send_x(kind, slot, ahead)
            if kind > 0:
                send_x(kind, slot, xp)

    def ring_step(t):
        ring(t, 1, xl)
        ring(t, 0, xl)
        ring(t, 2, xl)
        ring(t, 0, 1 - xl)

    def project(slot):
        block = xbuf[slot]
        start = pl.multiple_of(slot * COLS, COLS)
        q_sum[...] += jnp.dot(block, wq[pl.ds(start, COLS), :], preferred_element_type=jnp.float32)
        kv_sum[...] += lax.dot_general(
            wkv[:, pl.ds(start, COLS)], block, NT, preferred_element_type=jnp.float32
        )

    def steps(t):
        return (0,) if t == 0 else ((4,) if t == 4 else (t, -t))

    def own_column(t):
        for step in steps(t):
            project(head_at(xl, z - step))

    def other_column(t):
        for step in steps(t):
            slot = head_at(1 - xl, z - step)
            wait_x(1, slot)
            wait_x(2, slot)
            project(slot)

    def kv_start():
        k_in.wait()
        v_in.wait()
        for device in (yp, ym, sib):
            send_kv(yy, bit, pp, device)

    def kv_pair():
        send_kv(yy, bit, pp, pair)

    def kv_own_halves():
        wait_kv(yy, away, pp)
        for device in (yp, ym, sib):
            send_kv(yy, away, pp, device)

    def kv_forward(half):
        step = 2 * half - 1
        wait_kv(line(step), half, pp)
        send_kv(line(step), half, pp, (ctx_at(yy - step, pp), h))
        send_kv(line(step), half, pp, sib)

    def kv_rest(half):
        step = 1 - 2 * half
        wait_kv(line(step), half, pp)
        send_kv(line(step), half, pp, sib)

    def kv_opposite(half):
        wait_kv(line(2), half, pp)
        send_kv(line(2), half, pp, sib)

    def tables():
        angles = turn_ref[...] * position.astype(jnp.float32)
        cosine, sine = jnp.cos(angles), jnp.sin(angles)
        cos_k[...] = cosine
        sin_k[...] = sine
        cos_q[...] = jnp.concatenate([cosine, cosine], axis=0).T
        sin_q[...] = jnp.concatenate([-sine, sine], axis=0).T
        query_pos[0] = jnp.broadcast_to(position.astype(jnp.float32), (ROWS, ROWS)).T
        q_sum[...] = jnp.zeros_like(q_sum)
        kv_sum[...] = jnp.zeros_like(kv_sum)
        top[...] = jnp.full_like(top, NEGATIVE)
        total[...] = jnp.zeros_like(total)
        acc[...] = jnp.zeros_like(acc)

    first_wave()
    kv_start()
    remote(places.at[0], places.at[1], one_sem.at[0], far)
    second_wave()
    tables()
    ring_step(1)
    wk_in.wait()
    wv_in.wait()
    for copy in wq_in:
        copy.wait()
    own_column(0)
    ring_step(2)
    kv_pair()
    kv_forward(bit)
    kv_rest(bit)
    other_column(0)
    own_column(1)
    ring_step(3)
    other_column(1)
    own_column(2)
    ring_step(4)
    kv_own_halves()
    other_column(2)
    own_column(3)
    own_column(4)
    other_column(3)
    other_column(4)

    raw[bit] = kv_sum[...].astype(jnp.bfloat16)
    remote(raw.at[bit], raw.at[bit], one_sem.at[1], pair)
    cosine, sine = cos_q[...], sin_q[...]
    scale = HEAD**-0.5 * LOG2E
    for j in range(4):
        part = q_sum[:, HEAD * j : HEAD * (j + 1)]
        turned = part * cosine + pltpu.roll(part, HALF, 1) * sine
        qs[0, ROWS * j : ROWS * (j + 1), :] = (turned * scale).astype(jnp.bfloat16)
    remote(qs.at[0], qs.at[1], one_sem.at[2], far)

    def new_rows():
        arrived(raw.at[away], one_sem.at[1])
        low, high = raw[0, 0:HALF, :].astype(jnp.float32), raw[1, 0:HALF, :].astype(jnp.float32)
        cosine, sine = cos_k[...], sin_k[...]
        slot = yy * 2 + pp
        kvn[slot, 0:HALF, :] = (low * cosine - high * sine).astype(jnp.bfloat16)
        kvn[slot, HALF:HEAD, :] = (high * cosine + low * sine).astype(jnp.bfloat16)
        kvn[slot, HEAD : HEAD + HALF, :] = raw[0, HALF:HEAD, :]
        kvn[slot, HEAD + HALF : 2 * HEAD, :] = raw[1, HALF:HEAD, :]
        for device in (yp, ym, sib):
            send_new(yy, pp, device)

    def new_from_sides():
        wait_new(line(-1), pp)
        send_new(line(-1), pp, yp)
        send_new(line(-1), pp, sib)
        wait_new(line(1), pp)
        send_new(line(1), pp, sib)

    def new_opposite():
        wait_new(line(2), pp)
        send_new(line(2), pp, sib)

    def soften(which, r, tiles, values):
        rows = slice(PART * r, PART * (r + 1))
        before = top[which, rows]
        highest = tiles[0]
        for tile in tiles[1:]:
            highest = jnp.maximum(highest, tile)
        now = jnp.maximum(before, jnp.max(highest, axis=1, keepdims=True))
        factor = jnp.exp2(before - now)
        weights = [jnp.exp2(tile - now) for tile in tiles]
        added = weights[0]
        for weight in weights[1:]:
            added = added + weight
        total[which, rows] = total[which, rows] * factor + added
        top[which, rows] = now
        packed = jnp.concatenate([weight.astype(jnp.bfloat16) for weight in weights], axis=1)
        acc[which, rows] = acc[which, rows] * factor + lax.dot_general(
            packed, values, NT, preferred_element_type=jnp.float32
        )

    def split(scores):
        return [scores[:, 128 * j : 128 * (j + 1)] for j in range(scores.shape[1] // 128)]

    def scores(which, row, r):
        keys = jnp.concatenate([kvc[row, 0, 0:HALF, :], kvc[row, 1, 0:HALF, :]], axis=0)
        return jnp.dot(qs[which, PART * r : PART * (r + 1), :], keys, preferred_element_type=jnp.float32)

    def cached_values(row):
        return jnp.concatenate([kvc[row, 0, HALF:HEAD, :], kvc[row, 1, HALF:HEAD, :]], axis=0)

    def job(i):
        late = i // 4
        which = (1 - late) * (i % 2) + late * (1 - i % 4 // 2)
        return which, line((1 - late) * (i // 2) + late * (3 - i % 2))

    def new_scores(which, r):
        keys = jnp.concatenate([kvn[s, 0:HEAD, :] for s in range(2 * LINES)], axis=1)
        return jnp.dot(qs[which, PART * r : PART * (r + 1), :], keys, preferred_element_type=jnp.float32)

    def soften_new(which, r, found):
        asked = jnp.concatenate([query_pos[which]] * (PART // ROWS), axis=0)
        tiles = []
        for s, tile in enumerate(split(found)):
            code = kvn[s, 2 * HEAD :, :].astype(jnp.float32)
            tiles.append(jnp.where(code[0:1] * 256.0 + code[1:2] <= asked, tile, NEGATIVE))
        values = jnp.concatenate([kvn[s, HEAD : 2 * HEAD, :] for s in range(2 * LINES)], axis=1)
        soften(which, r, tiles, values)

    kv_opposite(bit)
    for half in (0, 1):
        wait_kv(yy, half, other)
    sbuf[0] = scores(0, yy, 0)

    @pl.loop(0, 6)
    def _(i):
        @pl.when(i == 0)
        def _():
            new_rows()
            kv_forward(away)
            arrived(qs.at[1], one_sem.at[2])

        @pl.when(i == 1)
        def _():
            kv_rest(away)
            for half in (0, 1):
                wait_kv(line(1), half, other)

        @pl.when(i == 2)
        def _():
            new_from_sides()

        @pl.when(i == 3)
        def _():
            kv_opposite(away)
            for half in (0, 1):
                wait_kv(line(3), half, other)

        @pl.when(i == 4)
        def _():
            new_opposite()
            for half in (0, 1):
                wait_kv(line(2), half, other)

        which, row = job(i)
        found = sbuf[0]
        sbuf[1] = scores(which, row, 1)
        values = cached_values(row)
        soften(which, 0, split(found), values)
        found = sbuf[1]
        next_which, next_row = job(i + 1)
        sbuf[0] = scores(next_which, next_row, 0)
        soften(which, 1, split(found), values)

    arrived(places.at[1], one_sem.at[0])
    code = places[1].astype(jnp.float32)
    query_pos[1] = jnp.broadcast_to(code[0:1] * 256.0 + code[1:2], (ROWS, ROWS)).T
    for step in range(LINES):
        wait_new(line(step), other)
    nbuf[0] = new_scores(1, 0)
    nbuf[1] = new_scores(1, 1)
    soften_new(1, 0, nbuf[0])
    soften_new(1, 1, nbuf[1])
    o_out[...] = acc[1].astype(jnp.bfloat16)
    lane = lax.broadcasted_iota(jnp.int32, (ROWS, HEAD), 1)
    state = jnp.zeros((ROWS, HEAD), jnp.float32)
    for j in range(4):
        rows = slice(ROWS * j, ROWS * (j + 1))
        state = jnp.where(lane == j, top[1, rows, :], state)
        state = jnp.where(lane == 4 + j, jnp.sum(total[1, rows, :], axis=1, keepdims=True), state)
    st_out[...] = state
    remote(st_out, st_in, one_sem.at[3], far)
    remote(o_out, o_in, one_sem.at[4], far)

    nbuf[0] = new_scores(0, 0)
    nbuf[1] = new_scores(0, 1)
    for i in (6, 7):
        which, row = 0, line(9 - i)
        found = sbuf[0]
        sbuf[1] = scores(which, row, 1)
        values = cached_values(row)
        soften(which, 0, split(found), values)
        found = sbuf[1]
        if i == 6:
            sbuf[0] = scores(0, line(2), 0)
        soften(which, 1, split(found), values)
    soften_new(0, 0, nbuf[0])
    soften_new(0, 1, nbuf[1])

    arrived(st_in, one_sem.at[3])
    arrived(o_in, one_sem.at[4])
    state = st_in[...]
    for j in range(4):
        rows = slice(ROWS * j, ROWS * (j + 1))
        here, there = top[0, rows, :], state[:, j : j + 1]
        both = jnp.maximum(here, there)
        near_part, far_part = jnp.exp2(here - both), jnp.exp2(there - both)
        near_sum = jnp.sum(total[0, rows, :], axis=1, keepdims=True)
        weight_sum = near_sum * near_part + state[:, 4 + j : 5 + j] * far_part
        mixed = acc[0, rows, :] * near_part + o_in[rows, :].astype(jnp.float32) * far_part
        out_ref[:, HEAD * j : HEAD * (j + 1)] = (mixed / weight_sum).astype(jnp.bfloat16)

    for number, like in enumerate(pending):
        ref = like()
        pltpu.make_async_remote_copy(
            src_ref=ref, dst_ref=ref, send_sem=send_sem.at[number], recv_sem=one_sem.at[0],
            device_id=sib, device_id_type=MESH,
        ).wait_send()


def per_device(
    new_states, query_weight, key_weight, value_weight, cache_keys, cache_values, new_positions
):
    turn = THETA ** (np.arange(HALF) * (-2.0 / HEAD))
    turn = jnp.asarray(np.repeat(turn[:, None], ROWS, axis=1), jnp.float32)
    hbm = pl.BlockSpec(memory_space=pl.ANY)
    vmem = pl.BlockSpec(memory_space=pltpu.VMEM)
    dma = pltpu.SemaphoreType.DMA
    bf16, f32 = jnp.bfloat16, jnp.float32
    scratch = [
        ((16, ROWS, COLS), bf16),
        ((8192, COLS), bf16),
        ((HEAD, 8192), bf16),
        ((LINES, 2, HEAD, 2 * CACHE), bf16),
        ((2 * LINES, 2 * HEAD + 16, ROWS), bf16),
        ((2, HEAD, ROWS), bf16),
        ((2, QROWS, HEAD), bf16),
        ((2, 16, ROWS), bf16),
        ((ROWS, COLS), f32),
        ((HEAD, ROWS), f32),
        ((2, QROWS, HEAD), f32),
        ((2, QROWS, HEAD), f32),
        ((2, QROWS, HEAD), f32),
        ((2, PART, 2 * CACHE), f32),
        ((2, PART, 2 * LINES * ROWS), f32),
        ((ROWS, HEAD), f32),
        ((ROWS, HEAD), f32),
        ((HALF, ROWS), f32),
        ((HALF, ROWS), f32),
        ((2, ROWS, HEAD), f32),
        ((QROWS, HEAD), bf16),
        ((QROWS, HEAD), bf16),
        ((ROWS, HEAD), f32),
        ((ROWS, HEAD), f32),
    ]
    return pl.pallas_call(
        kernel,
        out_shape=jax.ShapeDtypeStruct((ROWS, COLS), bf16),
        in_specs=[hbm] * 6 + [vmem] * 2,
        out_specs=vmem,
        scratch_shapes=[pltpu.VMEM(shape, kind) for shape, kind in scratch]
        + [dma((9,)), dma((3, 16)), dma((LINES, 2, 2)), dma((2 * LINES,)), dma((5,)), dma((SENDS,))],
        compiler_params=pltpu.CompilerParams(
            collective_id=0, has_side_effects=True, vmem_limit_bytes=56 << 20
        ),
    )(
        new_states, query_weight, key_weight.T, value_weight.T, cache_keys.T, cache_values.T,
        new_positions.reshape(1, ROWS), turn,
    )


def solution(mesh):
    placed = (
        P("ctx", "head"),
        P(None, "head"),
        P(None, "head"),
        P(None, "head"),
        P("ctx", "head"),
        P("ctx", "head"),
        P("ctx"),
    )
    return jax.shard_map(
        per_device, mesh=mesh, in_specs=placed, out_specs=P("ctx", "head"), check_vma=False
    )
```

```python
import math

import jax
import jax.numpy as jnp
import numpy as np
from jax import lax
from jax.experimental import pallas as pl
from jax.experimental.pallas import tpu as pltpu
from jax.sharding import PartitionSpec as P

THETA = 500000.0
NEGATIVE = -1e30
MESH = pl.DeviceIdType.MESH
LOG2E = math.log2(math.e)

ROWS = 128
COLS = 512
HEAD = 128
HALF = 64
CACHE = 1152
QROWS = 512
PART = 256
LINES = 4
SENDS = 120
CHUNKS = 3
CHUNK = 384
CUTS = ((0, 128), (128, 384), (384, 512))
REACH = {(0, 1): 4, (0, -1): 3, (1, 1): 3, (1, -1): 4, (2, 1): 4, (2, -1): 3}
NT = (((1,), (1,)), ((), ()))


def kernel(
    x_hbm, wq_hbm, wk_hbm, wv_hbm, ck_hbm, cv_hbm, pos_ref, turn_ref,
    out_ref,
    xbuf, wq, wkv, kvc, kvn, raw, qs, places, q_sum, kv_sum, top, total, acc, sbuf, nbuf,
    cos_q, sin_q, cos_k, sin_k, query_pos, o_out, o_in, st_out, st_in,
    local_sem, x_sem, kv_sem, kvn_sem, one_sem, send_sem,
):
    c = lax.axis_index("ctx")
    h = lax.axis_index("head")
    xh, yy, pp = c // 8, (c // 2) % 4, c % 2
    xl, z = h // 8, h % 8
    bit = h % 2
    away = 1 - bit
    other = 1 - pp

    def head_at(col, row):
        return col * 8 + (row + 8) % 8

    def ctx_at(row, core):
        return xh * 8 + ((row + 4) % 4) * 2 + core

    def line(step):
        return (yy + step + 4) % 4

    zp, zm = (c, head_at(xl, z + 1)), (c, head_at(xl, z - 1))
    xp = (c, head_at(1 - xl, z))
    pair = (c, h + 1 - 2 * bit)
    yp, ym = (ctx_at(yy + 1, pp), h), (ctx_at(yy - 1, pp), h)
    sib = (ctx_at(yy, other), h)
    far = ((c + 8) % 16, h)

    pending = []

    def remote(src, dst, sem, device, like=None):
        number = len(pending)
        pltpu.make_async_remote_copy(
            src_ref=src, dst_ref=dst, send_sem=send_sem.at[number], recv_sem=sem,
            device_id=device, device_id_type=MESH,
        ).start()
        pending.append(like or (lambda: src))

    def arrived(ref, sem):
        pltpu.make_async_remote_copy(
            src_ref=ref, dst_ref=ref, send_sem=send_sem.at[0], recv_sem=sem,
            device_id=sib, device_id_type=MESH,
        ).wait_recv()

    def local(i, src, dst):
        copy = pltpu.make_async_copy(src, dst, local_sem.at[i])
        copy.start()
        return copy

    def cached(row, half, core, k):
        return kvc.at[row, half, :, pl.ds(pl.multiple_of(core * CACHE + k * CHUNK, 128), CHUNK)]

    own = pl.ds(pl.multiple_of(pp * CACHE, 128), CACHE)
    x_in = local(0, x_hbm, xbuf.at[h])
    k_in = local(1, ck_hbm, kvc.at[yy, bit, 0:HALF, own])
    v_in = local(2, cv_hbm, kvc.at[yy, bit, HALF:HEAD, own])
    wk_in = local(3, wk_hbm, wkv.at[0:HALF, :])
    wv_in = local(4, wv_hbm, wkv.at[HALF:HEAD, :])
    wq_in = [
        local(5 + i, wq_hbm.at[2048 * i : 2048 * (i + 1), :], wq.at[2048 * i : 2048 * (i + 1), :])
        for i in range(4)
    ]

    barrier = pltpu.get_barrier_semaphore()
    for device in (zp, zm, xp, yp, ym, sib, far):
        pl.semaphore_signal(barrier, inc=1, device_id=device, device_id_type=MESH)

    position = pos_ref[...]
    row_index = lax.broadcasted_iota(jnp.int32, (16, ROWS), 0)
    coarse = jnp.broadcast_to((position // 256).astype(jnp.float32), (16, ROWS))
    fine = jnp.broadcast_to((position % 256).astype(jnp.float32), (16, ROWS))
    places[0] = jnp.where(row_index == 0, coarse, jnp.where(row_index == 1, fine, 0.0)).astype(jnp.bfloat16)
    kvn[yy * 2 + pp, 2 * HEAD :, :] = places[0]
    pl.semaphore_wait(barrier, 7)

    def piece(kind, slot):
        return xbuf.at[slot, :, CUTS[kind][0] : CUTS[kind][1]]

    def send_x(kind, slot, device):
        remote(piece(kind, slot), piece(kind, slot), x_sem.at[kind, slot], device)

    def wait_x(kind, slot):
        arrived(piece(kind, slot), x_sem.at[kind, slot])

    def send_kv(row, half, core, k, device):
        block = cached(row, half, core, k)
        remote(block, block, kv_sem.at[row, half, core * CHUNKS + k], device, lambda: kvc.at[0, 0, :, 0:CHUNK])

    def wait_kv(row, half, core, k):
        arrived(cached(row, half, core, k), kv_sem.at[row, half, core * CHUNKS + k])

    def wait_row(row):
        for half in (0, 1):
            for k in range(CHUNKS):
                wait_kv(row, half, other, k)

    def send_new(row, core, device):
        slot = row * 2 + core
        remote(kvn.at[slot], kvn.at[slot], kvn_sem.at[slot], device, lambda: kvn.at[0])

    def wait_new(row, core):
        slot = row * 2 + core
        arrived(kvn.at[slot], kvn_sem.at[slot])

    across = head_at(1 - xl, z)

    def first_wave():
        x_in.wait()
        send_x(0, h, xp)
        for kind in (1, 0):
            send_x(kind, h, zp)
            send_x(kind, h, zm)
        send_x(1, h, xp)

    def second_wave():
        send_x(2, h, zp)
        send_x(2, h, zm)
        send_x(2, h, xp)
        wait_x(0, across)
        send_x(0, across, zp)
        send_x(0, across, zm)

    def ring(t, kind, col):
        for sign, ahead in ((1, zp), (-1, zm)):
            last = REACH[kind, sign]
            if t > last:
                continue
            slot = head_at(col, z - sign * t)
            wait_x(kind, slot)
            if t < last:
                send_x(kind, slot, ahead)
            if kind > 0:
                send_x(kind, slot, xp)

    def ring_step(t):
        ring(t, 1, xl)
        ring(t, 0, xl)
        ring(t, 2, xl)
        ring(t, 0, 1 - xl)

    def project(slot):
        block = xbuf[slot]
        start = pl.multiple_of(slot * COLS, COLS)
        q_sum[...] += jnp.dot(block, wq[pl.ds(start, COLS), :], preferred_element_type=jnp.float32)
        kv_sum[...] += lax.dot_general(
            wkv[:, pl.ds(start, COLS)], block, NT, preferred_element_type=jnp.float32
        )

    def steps(t):
        return (0,) if t == 0 else ((4,) if t == 4 else (t, -t))

    def own_column(t):
        for step in steps(t):
            project(head_at(xl, z - step))

    def other_column(t):
        for step in steps(t):
            slot = head_at(1 - xl, z - step)
            wait_x(1, slot)
            wait_x(2, slot)
            project(slot)

    def kv_start():
        k_in.wait()
        v_in.wait()
        for k in range(CHUNKS):
            for device in (yp, ym, sib):
                send_kv(yy, bit, pp, k, device)

    def kv_pair(k):
        send_kv(yy, bit, pp, k, pair)

    def kv_own_halves(k):
        wait_kv(yy, away, pp, k)
        for device in (yp, ym, sib):
            send_kv(yy, away, pp, k, device)

    def kv_forward(half, k):
        step = 2 * half - 1
        wait_kv(line(step), half, pp, k)
        send_kv(line(step), half, pp, k, (ctx_at(yy - step, pp), h))
        send_kv(line(step), half, pp, k, sib)

    def kv_rest(half, k):
        step = 1 - 2 * half
        wait_kv(line(step), half, pp, k)
        send_kv(line(step), half, pp, k, sib)

    def kv_opposite(half, k):
        wait_kv(line(2), half, pp, k)
        send_kv(line(2), half, pp, k, sib)

    def tables():
        angles = turn_ref[...] * position.astype(jnp.float32)
        cosine, sine = jnp.cos(angles), jnp.sin(angles)
        cos_k[...] = cosine
        sin_k[...] = sine
        cos_q[...] = jnp.concatenate([cosine, cosine], axis=0).T
        sin_q[...] = jnp.concatenate([-sine, sine], axis=0).T
        query_pos[0] = jnp.broadcast_to(position.astype(jnp.float32), (ROWS, ROWS)).T
        q_sum[...] = jnp.zeros_like(q_sum)
        kv_sum[...] = jnp.zeros_like(kv_sum)
        top[...] = jnp.full_like(top, NEGATIVE)
        total[...] = jnp.zeros_like(total)
        acc[...] = jnp.zeros_like(acc)

    first_wave()
    kv_start()
    remote(places.at[0], places.at[1], one_sem.at[0], far)
    second_wave()
    kv_pair(0)
    tables()
    ring_step(1)
    kv_pair(1)
    wk_in.wait()
    wv_in.wait()
    for copy in wq_in:
        copy.wait()
    own_column(0)
    ring_step(2)
    kv_pair(2)
    kv_own_halves(0)
    for k in range(CHUNKS):
        kv_forward(bit, k)
    for k in range(CHUNKS):
        kv_rest(bit, k)
    other_column(0)
    own_column(1)
    ring_step(3)
    kv_own_halves(1)
    kv_forward(away, 0)
    other_column(1)
    own_column(2)
    ring_step(4)
    kv_own_halves(2)
    kv_forward(away, 1)
    kv_rest(away, 0)
    other_column(2)
    own_column(3)
    own_column(4)
    other_column(3)
    other_column(4)

    raw[bit] = kv_sum[...].astype(jnp.bfloat16)
    remote(raw.at[bit], raw.at[bit], one_sem.at[1], pair)
    cosine, sine = cos_q[...], sin_q[...]
    scale = HEAD**-0.5 * LOG2E
    for j in range(4):
        part = q_sum[:, HEAD * j : HEAD * (j + 1)]
        turned = part * cosine + pltpu.roll(part, HALF, 1) * sine
        qs[0, ROWS * j : ROWS * (j + 1), :] = (turned * scale).astype(jnp.bfloat16)
    remote(qs.at[0], qs.at[1], one_sem.at[2], far)

    def new_rows():
        arrived(raw.at[away], one_sem.at[1])
        low, high = raw[0, 0:HALF, :].astype(jnp.float32), raw[1, 0:HALF, :].astype(jnp.float32)
        cosine, sine = cos_k[...], sin_k[...]
        slot = yy * 2 + pp
        kvn[slot, 0:HALF, :] = (low * cosine - high * sine).astype(jnp.bfloat16)
        kvn[slot, HALF:HEAD, :] = (high * cosine + low * sine).astype(jnp.bfloat16)
        kvn[slot, HEAD : HEAD + HALF, :] = raw[0, HALF:HEAD, :]
        kvn[slot, HEAD + HALF : 2 * HEAD, :] = raw[1, HALF:HEAD, :]
        for device in (yp, ym, sib):
            send_new(yy, pp, device)

    def new_from_sides():
        wait_new(line(-1), pp)
        send_new(line(-1), pp, yp)
        send_new(line(-1), pp, sib)
        wait_new(line(1), pp)
        send_new(line(1), pp, sib)

    def new_opposite():
        wait_new(line(2), pp)
        send_new(line(2), pp, sib)

    def soften(which, r, tiles, values):
        rows = slice(PART * r, PART * (r + 1))
        before = top[which, rows]
        highest = tiles[0]
        for tile in tiles[1:]:
            highest = jnp.maximum(highest, tile)
        now = jnp.maximum(before, jnp.max(highest, axis=1, keepdims=True))
        factor = jnp.exp2(before - now)
        weights = [jnp.exp2(tile - now) for tile in tiles]
        added = weights[0]
        for weight in weights[1:]:
            added = added + weight
        total[which, rows] = total[which, rows] * factor + added
        top[which, rows] = now
        packed = jnp.concatenate([weight.astype(jnp.bfloat16) for weight in weights], axis=1)
        acc[which, rows] = acc[which, rows] * factor + lax.dot_general(
            packed, values, NT, preferred_element_type=jnp.float32
        )

    def split(scores):
        return [scores[:, 128 * j : 128 * (j + 1)] for j in range(scores.shape[1] // 128)]

    def scores(which, row, r):
        keys = jnp.concatenate([kvc[row, 0, 0:HALF, :], kvc[row, 1, 0:HALF, :]], axis=0)
        return jnp.dot(qs[which, PART * r : PART * (r + 1), :], keys, preferred_element_type=jnp.float32)

    def cached_values(row):
        return jnp.concatenate([kvc[row, 0, HALF:HEAD, :], kvc[row, 1, HALF:HEAD, :]], axis=0)

    def job(i):
        which = (i + 3) // 4 % 2
        turn = (i + 3) % 4 * which + i // 5
        step = turn * (1 - turn // 2) + turn // 2 * (5 - turn)
        return which, line(step)

    def new_scores(which, r):
        keys = jnp.concatenate([kvn[s, 0:HEAD, :] for s in range(2 * LINES)], axis=1)
        return jnp.dot(qs[which, PART * r : PART * (r + 1), :], keys, preferred_element_type=jnp.float32)

    def soften_new(which, r, found):
        asked = jnp.concatenate([query_pos[which]] * (PART // ROWS), axis=0)
        tiles = []
        for s, tile in enumerate(split(found)):
            code = kvn[s, 2 * HEAD :, :].astype(jnp.float32)
            tiles.append(jnp.where(code[0:1] * 256.0 + code[1:2] <= asked, tile, NEGATIVE))
        values = jnp.concatenate([kvn[s, HEAD : 2 * HEAD, :] for s in range(2 * LINES)], axis=1)
        soften(which, r, tiles, values)

    for k in range(CHUNKS):
        kv_opposite(bit, k)
    wait_row(yy)
    sbuf[0] = scores(0, yy, 0)

    @pl.loop(0, 5)
    def _(i):
        @pl.when(i == 0)
        def _():
            new_rows()
            kv_forward(away, 2)
            kv_rest(away, 1)
            arrived(qs.at[1], one_sem.at[2])

        @pl.when(i == 1)
        def _():
            kv_rest(away, 2)
            wait_row(line(1))
            new_from_sides()

        @pl.when(i == 2)
        def _():
            for k in range(CHUNKS):
                kv_opposite(away, k)
            wait_row(line(3))

        @pl.when(i == 3)
        def _():
            new_opposite()
            wait_row(line(2))

        which, row = job(i)
        found = sbuf[0]
        sbuf[1] = scores(which, row, 1)
        values = cached_values(row)
        soften(which, 0, split(found), values)
        found = sbuf[1]
        next_which, next_row = job(i + 1)
        sbuf[0] = scores(next_which, next_row, 0)
        soften(which, 1, split(found), values)

    arrived(places.at[1], one_sem.at[0])
    code = places[1].astype(jnp.float32)
    query_pos[1] = jnp.broadcast_to(code[0:1] * 256.0 + code[1:2], (ROWS, ROWS)).T
    for step in range(LINES):
        wait_new(line(step), other)
    nbuf[0] = new_scores(1, 0)
    nbuf[1] = new_scores(1, 1)
    soften_new(1, 0, nbuf[0])
    soften_new(1, 1, nbuf[1])
    o_out[...] = acc[1].astype(jnp.bfloat16)
    lane = lax.broadcasted_iota(jnp.int32, (ROWS, HEAD), 1)
    state = jnp.zeros((ROWS, HEAD), jnp.float32)
    for j in range(4):
        rows = slice(ROWS * j, ROWS * (j + 1))
        state = jnp.where(lane == j, top[1, rows, :], state)
        state = jnp.where(lane == 4 + j, jnp.sum(total[1, rows, :], axis=1, keepdims=True), state)
    st_out[...] = state
    remote(st_out, st_in, one_sem.at[3], far)
    remote(o_out, o_in, one_sem.at[4], far)

    nbuf[0] = new_scores(0, 0)
    nbuf[1] = new_scores(0, 1)
    for i, step in ((5, 1), (6, 3), (7, 2)):
        which, row = 0, line(step)
        found = sbuf[0]
        sbuf[1] = scores(which, row, 1)
        values = cached_values(row)
        soften(which, 0, split(found), values)
        found = sbuf[1]
        if i < 7:
            sbuf[0] = scores(0, line(4 - step if step == 1 else 2), 0)
        soften(which, 1, split(found), values)
    soften_new(0, 0, nbuf[0])
    soften_new(0, 1, nbuf[1])

    arrived(st_in, one_sem.at[3])
    arrived(o_in, one_sem.at[4])
    state = st_in[...]
    for j in range(4):
        rows = slice(ROWS * j, ROWS * (j + 1))
        here, there = top[0, rows, :], state[:, j : j + 1]
        both = jnp.maximum(here, there)
        near_part, far_part = jnp.exp2(here - both), jnp.exp2(there - both)
        near_sum = jnp.sum(total[0, rows, :], axis=1, keepdims=True)
        weight_sum = near_sum * near_part + state[:, 4 + j : 5 + j] * far_part
        mixed = acc[0, rows, :] * near_part + o_in[rows, :].astype(jnp.float32) * far_part
        out_ref[:, HEAD * j : HEAD * (j + 1)] = (mixed / weight_sum).astype(jnp.bfloat16)

    for number, like in enumerate(pending):
        ref = like()
        pltpu.make_async_remote_copy(
            src_ref=ref, dst_ref=ref, send_sem=send_sem.at[number], recv_sem=one_sem.at[0],
            device_id=sib, device_id_type=MESH,
        ).wait_send()


def per_device(
    new_states, query_weight, key_weight, value_weight, cache_keys, cache_values, new_positions
):
    turn = THETA ** (np.arange(HALF) * (-2.0 / HEAD))
    turn = jnp.asarray(np.repeat(turn[:, None], ROWS, axis=1), jnp.float32)
    hbm = pl.BlockSpec(memory_space=pl.ANY)
    vmem = pl.BlockSpec(memory_space=pltpu.VMEM)
    dma = pltpu.SemaphoreType.DMA
    bf16, f32 = jnp.bfloat16, jnp.float32
    scratch = [
        ((16, ROWS, COLS), bf16),
        ((8192, COLS), bf16),
        ((HEAD, 8192), bf16),
        ((LINES, 2, HEAD, 2 * CACHE), bf16),
        ((2 * LINES, 2 * HEAD + 16, ROWS), bf16),
        ((2, HEAD, ROWS), bf16),
        ((2, QROWS, HEAD), bf16),
        ((2, 16, ROWS), bf16),
        ((ROWS, COLS), f32),
        ((HEAD, ROWS), f32),
        ((2, QROWS, HEAD), f32),
        ((2, QROWS, HEAD), f32),
        ((2, QROWS, HEAD), f32),
        ((2, PART, 2 * CACHE), f32),
        ((2, PART, 2 * LINES * ROWS), f32),
        ((ROWS, HEAD), f32),
        ((ROWS, HEAD), f32),
        ((HALF, ROWS), f32),
        ((HALF, ROWS), f32),
        ((2, ROWS, HEAD), f32),
        ((QROWS, HEAD), bf16),
        ((QROWS, HEAD), bf16),
        ((ROWS, HEAD), f32),
        ((ROWS, HEAD), f32),
    ]
    return pl.pallas_call(
        kernel,
        out_shape=jax.ShapeDtypeStruct((ROWS, COLS), bf16),
        in_specs=[hbm] * 6 + [vmem] * 2,
        out_specs=vmem,
        scratch_shapes=[pltpu.VMEM(shape, kind) for shape, kind in scratch]
        + [dma((9,)), dma((3, 16)), dma((LINES, 2, 2 * CHUNKS)), dma((2 * LINES,)), dma((5,)), dma((SENDS,))],
        compiler_params=pltpu.CompilerParams(
            collective_id=0, has_side_effects=True, vmem_limit_bytes=56 << 20
        ),
    )(
        new_states, query_weight, key_weight.T, value_weight.T, cache_keys.T, cache_values.T,
        new_positions.reshape(1, ROWS), turn,
    )


def solution(mesh):
    placed = (
        P("ctx", "head"),
        P(None, "head"),
        P(None, "head"),
        P(None, "head"),
        P("ctx", "head"),
        P("ctx", "head"),
        P("ctx"),
    )
    return jax.shard_map(
        per_device, mesh=mesh, in_specs=placed, out_specs=P("ctx", "head"), check_vma=False
    )
```

```python
import math

import jax
import jax.numpy as jnp
import numpy as np
from jax import lax
from jax.experimental import pallas as pl
from jax.experimental.pallas import tpu as pltpu
from jax.sharding import PartitionSpec as P

THETA = 500000.0
NEGATIVE = -1e30
MESH = pl.DeviceIdType.MESH
LOG2E = math.log2(math.e)

ROWS = 128
COLS = 512
HEAD = 128
HALF = 64
CACHE = 1152
QROWS = 512
PART = 256
LINES = 4
SENDS = 120
CHUNKS = 3
CHUNK = 384
CUTS = ((0, 128), (128, 384), (384, 512))
REACH = {(0, 1): 4, (0, -1): 3, (1, 1): 3, (1, -1): 4, (2, 1): 4, (2, -1): 3}
NT = (((1,), (1,)), ((), ()))


def kernel(
    x_hbm, wq_hbm, wk_hbm, wv_hbm, ck_hbm, cv_hbm, pos_ref, turn_ref,
    out_ref,
    xbuf, wq, wkv, kvc, kvn, raw, qs, places, q_sum, kv_sum, top, total, acc, sbuf, nbuf,
    cos_q, sin_q, cos_k, sin_k, query_pos, o_out, o_in, st_out, st_in,
    local_sem, x_sem, kv_sem, kvn_sem, one_sem, send_sem,
):
    c = lax.axis_index("ctx")
    h = lax.axis_index("head")
    xh, yy, pp = c // 8, (c // 2) % 4, c % 2
    xl, z = h // 8, h % 8
    bit = h % 2
    away = 1 - bit
    other = 1 - pp

    def head_at(col, row):
        return col * 8 + (row + 8) % 8

    def ctx_at(row, core):
        return xh * 8 + ((row + 4) % 4) * 2 + core

    def line(step):
        return (yy + step + 4) % 4

    zp, zm = (c, head_at(xl, z + 1)), (c, head_at(xl, z - 1))
    xp = (c, head_at(1 - xl, z))
    pair = (c, h + 1 - 2 * bit)
    yp, ym = (ctx_at(yy + 1, pp), h), (ctx_at(yy - 1, pp), h)
    sib = (ctx_at(yy, other), h)
    far = ((c + 8) % 16, h)

    pending = []

    def remote(src, dst, sem, device, like=None):
        number = len(pending)
        pltpu.make_async_remote_copy(
            src_ref=src, dst_ref=dst, send_sem=send_sem.at[number], recv_sem=sem,
            device_id=device, device_id_type=MESH,
        ).start()
        pending.append(like or (lambda: src))

    def arrived(ref, sem):
        pltpu.make_async_remote_copy(
            src_ref=ref, dst_ref=ref, send_sem=send_sem.at[0], recv_sem=sem,
            device_id=sib, device_id_type=MESH,
        ).wait_recv()

    settled = []

    def settle(end):
        for number in range(len(settled), end):
            ref = pending[number]()
            pltpu.make_async_remote_copy(
                src_ref=ref, dst_ref=ref, send_sem=send_sem.at[number], recv_sem=one_sem.at[0],
                device_id=sib, device_id_type=MESH,
            ).wait_send()
            settled.append(number)

    def local(i, src, dst):
        copy = pltpu.make_async_copy(src, dst, local_sem.at[i])
        copy.start()
        return copy

    def cached(row, half, core, k):
        return kvc.at[row, half, :, pl.ds(pl.multiple_of(core * CACHE + k * CHUNK, 128), CHUNK)]

    own = pl.ds(pl.multiple_of(pp * CACHE, 128), CACHE)
    x_in = local(0, x_hbm, xbuf.at[h])
    k_in = local(1, ck_hbm, kvc.at[yy, bit, 0:HALF, own])
    v_in = local(2, cv_hbm, kvc.at[yy, bit, HALF:HEAD, own])
    wk_in = local(3, wk_hbm, wkv.at[0:HALF, :])
    wv_in = local(4, wv_hbm, wkv.at[HALF:HEAD, :])
    wq_in = [
        local(5 + i, wq_hbm.at[2048 * i : 2048 * (i + 1), :], wq.at[2048 * i : 2048 * (i + 1), :])
        for i in range(4)
    ]

    barrier = pltpu.get_barrier_semaphore()
    for device in (zp, zm, xp, yp, ym, sib, far):
        pl.semaphore_signal(barrier, inc=1, device_id=device, device_id_type=MESH)

    position = pos_ref[...]
    row_index = lax.broadcasted_iota(jnp.int32, (16, ROWS), 0)
    coarse = jnp.broadcast_to((position // 256).astype(jnp.float32), (16, ROWS))
    fine = jnp.broadcast_to((position % 256).astype(jnp.float32), (16, ROWS))
    places[0] = jnp.where(row_index == 0, coarse, jnp.where(row_index == 1, fine, 0.0)).astype(jnp.bfloat16)
    kvn[yy * 2 + pp, 2 * HEAD :, :] = places[0]
    pl.semaphore_wait(barrier, 7)

    def piece(kind, slot):
        return xbuf.at[slot, :, CUTS[kind][0] : CUTS[kind][1]]

    def send_x(kind, slot, device):
        remote(piece(kind, slot), piece(kind, slot), x_sem.at[kind, slot], device)

    def wait_x(kind, slot):
        arrived(piece(kind, slot), x_sem.at[kind, slot])

    def send_kv(row, half, core, k, device):
        block = cached(row, half, core, k)
        remote(block, block, kv_sem.at[row, half, core * CHUNKS + k], device, lambda: kvc.at[0, 0, :, 0:CHUNK])

    def wait_kv(row, half, core, k):
        arrived(cached(row, half, core, k), kv_sem.at[row, half, core * CHUNKS + k])

    def wait_row(row):
        for half in (0, 1):
            for k in range(CHUNKS):
                wait_kv(row, half, other, k)

    def send_new(row, core, device):
        slot = row * 2 + core
        remote(kvn.at[slot], kvn.at[slot], kvn_sem.at[slot], device, lambda: kvn.at[0])

    def wait_new(row, core):
        slot = row * 2 + core
        arrived(kvn.at[slot], kvn_sem.at[slot])

    across = head_at(1 - xl, z)

    def first_wave():
        x_in.wait()
        send_x(0, h, xp)
        for kind in (1, 0):
            send_x(kind, h, zp)
            send_x(kind, h, zm)
        send_x(1, h, xp)

    def second_wave():
        send_x(2, h, zp)
        send_x(2, h, zm)
        send_x(2, h, xp)
        wait_x(0, across)
        send_x(0, across, zp)
        send_x(0, across, zm)

    def ring(t, kind, col):
        for sign, ahead in ((1, zp), (-1, zm)):
            last = REACH[kind, sign]
            if t > last:
                continue
            slot = head_at(col, z - sign * t)
            wait_x(kind, slot)
            if t < last:
                send_x(kind, slot, ahead)
            if kind > 0:
                send_x(kind, slot, xp)

    def ring_step(t):
        ring(t, 1, xl)
        ring(t, 0, xl)
        ring(t, 2, xl)
        ring(t, 0, 1 - xl)

    def project(slot):
        block = xbuf[slot]
        start = pl.multiple_of(slot * COLS, COLS)
        q_sum[...] += jnp.dot(block, wq[pl.ds(start, COLS), :], preferred_element_type=jnp.float32)
        kv_sum[...] += lax.dot_general(
            wkv[:, pl.ds(start, COLS)], block, NT, preferred_element_type=jnp.float32
        )

    def steps(t):
        return (0,) if t == 0 else ((4,) if t == 4 else (t, -t))

    def own_column(t):
        for step in steps(t):
            project(head_at(xl, z - step))

    def other_column(t):
        for step in steps(t):
            slot = head_at(1 - xl, z - step)
            wait_x(1, slot)
            wait_x(2, slot)
            project(slot)

    def kv_start():
        k_in.wait()
        v_in.wait()
        for k in range(CHUNKS):
            for device in (yp, ym, sib):
                send_kv(yy, bit, pp, k, device)

    def kv_pair(k):
        send_kv(yy, bit, pp, k, pair)

    def kv_own_halves(k):
        wait_kv(yy, away, pp, k)
        for device in (yp, ym, sib):
            send_kv(yy, away, pp, k, device)

    def kv_forward(half, k):
        step = 2 * half - 1
        wait_kv(line(step), half, pp, k)
        send_kv(line(step), half, pp, k, (ctx_at(yy - step, pp), h))
        send_kv(line(step), half, pp, k, sib)

    def kv_rest(half, k):
        step = 1 - 2 * half
        wait_kv(line(step), half, pp, k)
        send_kv(line(step), half, pp, k, sib)

    def kv_opposite(half, k):
        wait_kv(line(2), half, pp, k)
        send_kv(line(2), half, pp, k, sib)

    def tables():
        angles = turn_ref[...] * position.astype(jnp.float32)
        cosine, sine = jnp.cos(angles), jnp.sin(angles)
        cos_k[...] = cosine
        sin_k[...] = sine
        cos_q[...] = jnp.concatenate([cosine, cosine], axis=0).T
        sin_q[...] = jnp.concatenate([-sine, sine], axis=0).T
        query_pos[0] = jnp.broadcast_to(position.astype(jnp.float32), (ROWS, ROWS)).T
        q_sum[...] = jnp.zeros_like(q_sum)
        kv_sum[...] = jnp.zeros_like(kv_sum)
        top[...] = jnp.full_like(top, NEGATIVE)
        total[...] = jnp.zeros_like(total)
        acc[...] = jnp.zeros_like(acc)

    first_wave()
    kv_start()
    remote(places.at[0], places.at[1], one_sem.at[0], far)
    second_wave()
    kv_pair(0)
    first = len(pending)
    tables()
    ring_step(1)
    second = len(pending)
    kv_pair(1)
    wk_in.wait()
    wv_in.wait()
    for copy in wq_in:
        copy.wait()
    own_column(0)
    ring_step(2)
    kv_pair(2)
    kv_own_halves(0)
    for k in range(CHUNKS):
        kv_forward(bit, k)
    for k in range(CHUNKS):
        kv_rest(bit, k)
    other_column(0)
    own_column(1)
    settle(first)
    ring_step(3)
    kv_own_halves(1)
    other_column(1)
    own_column(2)
    settle(second)
    ring_step(4)
    kv_own_halves(2)
    other_column(2)
    own_column(3)
    own_column(4)
    kv_forward(away, 0)
    other_column(3)
    other_column(4)

    raw[bit] = kv_sum[...].astype(jnp.bfloat16)
    remote(raw.at[bit], raw.at[bit], one_sem.at[1], pair)
    cosine, sine = cos_q[...], sin_q[...]
    scale = HEAD**-0.5 * LOG2E
    for j in range(4):
        part = q_sum[:, HEAD * j : HEAD * (j + 1)]
        turned = part * cosine + pltpu.roll(part, HALF, 1) * sine
        qs[0, ROWS * j : ROWS * (j + 1), :] = (turned * scale).astype(jnp.bfloat16)
    remote(qs.at[0], qs.at[1], one_sem.at[2], far)

    def new_rows():
        arrived(raw.at[away], one_sem.at[1])
        low, high = raw[0, 0:HALF, :].astype(jnp.float32), raw[1, 0:HALF, :].astype(jnp.float32)
        cosine, sine = cos_k[...], sin_k[...]
        slot = yy * 2 + pp
        kvn[slot, 0:HALF, :] = (low * cosine - high * sine).astype(jnp.bfloat16)
        kvn[slot, HALF:HEAD, :] = (high * cosine + low * sine).astype(jnp.bfloat16)
        kvn[slot, HEAD : HEAD + HALF, :] = raw[0, HALF:HEAD, :]
        kvn[slot, HEAD + HALF : 2 * HEAD, :] = raw[1, HALF:HEAD, :]
        for device in (yp, ym, sib):
            send_new(yy, pp, device)

    def new_from_sides():
        wait_new(line(-1), pp)
        send_new(line(-1), pp, yp)
        send_new(line(-1), pp, sib)
        wait_new(line(1), pp)
        send_new(line(1), pp, sib)

    def new_opposite():
        wait_new(line(2), pp)
        send_new(line(2), pp, sib)

    def soften(which, r, tiles, values):
        rows = slice(PART * r, PART * (r + 1))
        before = top[which, rows]
        highest = tiles[0]
        for tile in tiles[1:]:
            highest = jnp.maximum(highest, tile)
        now = jnp.maximum(before, jnp.max(highest, axis=1, keepdims=True))
        factor = jnp.exp2(before - now)
        weights = [jnp.exp2(tile - now) for tile in tiles]
        added = weights[0]
        for weight in weights[1:]:
            added = added + weight
        total[which, rows] = total[which, rows] * factor + added
        top[which, rows] = now
        packed = jnp.concatenate([weight.astype(jnp.bfloat16) for weight in weights], axis=1)
        acc[which, rows] = acc[which, rows] * factor + lax.dot_general(
            packed, values, NT, preferred_element_type=jnp.float32
        )

    def split(scores):
        return [scores[:, 128 * j : 128 * (j + 1)] for j in range(scores.shape[1] // 128)]

    def scores(which, row, r):
        keys = jnp.concatenate([kvc[row, 0, 0:HALF, :], kvc[row, 1, 0:HALF, :]], axis=0)
        return jnp.dot(qs[which, PART * r : PART * (r + 1), :], keys, preferred_element_type=jnp.float32)

    def cached_values(row):
        return jnp.concatenate([kvc[row, 0, HALF:HEAD, :], kvc[row, 1, HALF:HEAD, :]], axis=0)

    def job(i):
        which = (i + 3) // 4 % 2
        turn = (i + 3) % 4 * which + i // 5
        step = turn * (1 - turn // 2) + turn // 2 * (5 - turn)
        return which, line(step)

    def new_scores(which, r):
        keys = jnp.concatenate([kvn[s, 0:HEAD, :] for s in range(2 * LINES)], axis=1)
        return jnp.dot(qs[which, PART * r : PART * (r + 1), :], keys, preferred_element_type=jnp.float32)

    def soften_new(which, r, found):
        asked = jnp.concatenate([query_pos[which]] * (PART // ROWS), axis=0)
        tiles = []
        for s, tile in enumerate(split(found)):
            code = kvn[s, 2 * HEAD :, :].astype(jnp.float32)
            tiles.append(jnp.where(code[0:1] * 256.0 + code[1:2] <= asked, tile, NEGATIVE))
        values = jnp.concatenate([kvn[s, HEAD : 2 * HEAD, :] for s in range(2 * LINES)], axis=1)
        soften(which, r, tiles, values)

    for k in range(CHUNKS):
        kv_opposite(bit, k)
    wait_row(yy)
    sbuf[0] = scores(0, yy, 0)

    @pl.loop(0, 5)
    def _(i):
        @pl.when(i == 0)
        def _():
            new_rows()
            kv_forward(away, 1)
            kv_forward(away, 2)
            kv_rest(away, 0)
            kv_rest(away, 1)
            arrived(qs.at[1], one_sem.at[2])

        @pl.when(i == 1)
        def _():
            kv_rest(away, 2)
            wait_row(line(1))
            new_from_sides()

        @pl.when(i == 2)
        def _():
            for k in range(CHUNKS):
                kv_opposite(away, k)
            wait_row(line(3))

        @pl.when(i == 3)
        def _():
            new_opposite()
            wait_row(line(2))

        which, row = job(i)
        found = sbuf[0]
        sbuf[1] = scores(which, row, 1)
        values = cached_values(row)
        soften(which, 0, split(found), values)
        found = sbuf[1]
        next_which, next_row = job(i + 1)
        sbuf[0] = scores(next_which, next_row, 0)
        soften(which, 1, split(found), values)

    arrived(places.at[1], one_sem.at[0])
    code = places[1].astype(jnp.float32)
    query_pos[1] = jnp.broadcast_to(code[0:1] * 256.0 + code[1:2], (ROWS, ROWS)).T
    for step in range(LINES):
        wait_new(line(step), other)
    nbuf[0] = new_scores(1, 0)
    nbuf[1] = new_scores(1, 1)
    soften_new(1, 0, nbuf[0])
    soften_new(1, 1, nbuf[1])
    o_out[...] = acc[1].astype(jnp.bfloat16)
    lane = lax.broadcasted_iota(jnp.int32, (ROWS, HEAD), 1)
    state = jnp.zeros((ROWS, HEAD), jnp.float32)
    for j in range(4):
        rows = slice(ROWS * j, ROWS * (j + 1))
        state = jnp.where(lane == j, top[1, rows, :], state)
        state = jnp.where(lane == 4 + j, jnp.sum(total[1, rows, :], axis=1, keepdims=True), state)
    st_out[...] = state
    remote(st_out, st_in, one_sem.at[3], far)
    remote(o_out, o_in, one_sem.at[4], far)

    nbuf[0] = new_scores(0, 0)
    nbuf[1] = new_scores(0, 1)
    for i, step in ((5, 1), (6, 3), (7, 2)):
        which, row = 0, line(step)
        found = sbuf[0]
        sbuf[1] = scores(which, row, 1)
        values = cached_values(row)
        soften(which, 0, split(found), values)
        found = sbuf[1]
        if i < 7:
            sbuf[0] = scores(0, line(4 - step if step == 1 else 2), 0)
        soften(which, 1, split(found), values)
    soften_new(0, 0, nbuf[0])
    soften_new(0, 1, nbuf[1])

    settle(len(pending) - 2)
    arrived(st_in, one_sem.at[3])
    arrived(o_in, one_sem.at[4])
    state = st_in[...]
    for j in range(4):
        rows = slice(ROWS * j, ROWS * (j + 1))
        here, there = top[0, rows, :], state[:, j : j + 1]
        both = jnp.maximum(here, there)
        near_part, far_part = jnp.exp2(here - both), jnp.exp2(there - both)
        near_sum = jnp.sum(total[0, rows, :], axis=1, keepdims=True)
        weight_sum = near_sum * near_part + state[:, 4 + j : 5 + j] * far_part
        mixed = acc[0, rows, :] * near_part + o_in[rows, :].astype(jnp.float32) * far_part
        out_ref[:, HEAD * j : HEAD * (j + 1)] = (mixed / weight_sum).astype(jnp.bfloat16)

    settle(len(pending))


def per_device(
    new_states, query_weight, key_weight, value_weight, cache_keys, cache_values, new_positions
):
    turn = THETA ** (np.arange(HALF) * (-2.0 / HEAD))
    turn = jnp.asarray(np.repeat(turn[:, None], ROWS, axis=1), jnp.float32)
    hbm = pl.BlockSpec(memory_space=pl.ANY)
    vmem = pl.BlockSpec(memory_space=pltpu.VMEM)
    dma = pltpu.SemaphoreType.DMA
    bf16, f32 = jnp.bfloat16, jnp.float32
    scratch = [
        ((16, ROWS, COLS), bf16),
        ((8192, COLS), bf16),
        ((HEAD, 8192), bf16),
        ((LINES, 2, HEAD, 2 * CACHE), bf16),
        ((2 * LINES, 2 * HEAD + 16, ROWS), bf16),
        ((2, HEAD, ROWS), bf16),
        ((2, QROWS, HEAD), bf16),
        ((2, 16, ROWS), bf16),
        ((ROWS, COLS), f32),
        ((HEAD, ROWS), f32),
        ((2, QROWS, HEAD), f32),
        ((2, QROWS, HEAD), f32),
        ((2, QROWS, HEAD), f32),
        ((2, PART, 2 * CACHE), f32),
        ((2, PART, 2 * LINES * ROWS), f32),
        ((ROWS, HEAD), f32),
        ((ROWS, HEAD), f32),
        ((HALF, ROWS), f32),
        ((HALF, ROWS), f32),
        ((2, ROWS, HEAD), f32),
        ((QROWS, HEAD), bf16),
        ((QROWS, HEAD), bf16),
        ((ROWS, HEAD), f32),
        ((ROWS, HEAD), f32),
    ]
    return pl.pallas_call(
        kernel,
        out_shape=jax.ShapeDtypeStruct((ROWS, COLS), bf16),
        in_specs=[hbm] * 6 + [vmem] * 2,
        out_specs=vmem,
        scratch_shapes=[pltpu.VMEM(shape, kind) for shape, kind in scratch]
        + [dma((9,)), dma((3, 16)), dma((LINES, 2, 2 * CHUNKS)), dma((2 * LINES,)), dma((5,)), dma((SENDS,))],
        compiler_params=pltpu.CompilerParams(
            collective_id=0, has_side_effects=True, vmem_limit_bytes=56 << 20
        ),
    )(
        new_states, query_weight, key_weight.T, value_weight.T, cache_keys.T, cache_values.T,
        new_positions.reshape(1, ROWS), turn,
    )


def solution(mesh):
    placed = (
        P("ctx", "head"),
        P(None, "head"),
        P(None, "head"),
        P(None, "head"),
        P("ctx", "head"),
        P("ctx", "head"),
        P("ctx"),
    )
    return jax.shard_map(
        per_device, mesh=mesh, in_specs=placed, out_specs=P("ctx", "head"), check_vma=False
    )
```

```python
import math

import jax
import jax.numpy as jnp
import numpy as np
from jax import lax
from jax.experimental import pallas as pl
from jax.experimental.pallas import tpu as pltpu
from jax.sharding import PartitionSpec as P

THETA = 500000.0
NEGATIVE = -1e30
MESH = pl.DeviceIdType.MESH
LOG2E = math.log2(math.e)

ROWS = 128
COLS = 512
HEAD = 128
HALF = 64
CACHE = 1152
QROWS = 512
PART = 256
LINES = 4
SENDS = 120
CHUNKS = 3
CHUNK = 384
CUTS = ((0, 128), (128, 384), (384, 512))
REACH = {(0, 1): 4, (0, -1): 3, (1, 1): 3, (1, -1): 4, (2, 1): 4, (2, -1): 3}
NT = (((1,), (1,)), ((), ()))


def kernel(
    x_hbm, wq_hbm, wk_hbm, wv_hbm, ck_hbm, cv_hbm, pos_ref, turn_ref,
    out_ref,
    xbuf, wq, wkv, kvc, kvn, raw, qs, places, q_sum, kv_sum, top, total, acc, sbuf, nbuf,
    cos_q, sin_q, cos_k, sin_k, query_pos, o_out, o_in, st_out, st_in,
    local_sem, x_sem, kv_sem, kvn_sem, one_sem, send_sem,
):
    c = lax.axis_index("ctx")
    h = lax.axis_index("head")
    xh, yy, pp = c // 8, (c // 2) % 4, c % 2
    xl, z = h // 8, h % 8
    bit = h % 2
    away = 1 - bit
    other = 1 - pp

    def head_at(col, row):
        return col * 8 + (row + 8) % 8

    def ctx_at(row, core):
        return xh * 8 + ((row + 4) % 4) * 2 + core

    def line(step):
        return (yy + step + 4) % 4

    zp, zm = (c, head_at(xl, z + 1)), (c, head_at(xl, z - 1))
    xp = (c, head_at(1 - xl, z))
    pair = (c, h + 1 - 2 * bit)
    yp, ym = (ctx_at(yy + 1, pp), h), (ctx_at(yy - 1, pp), h)
    sib = (ctx_at(yy, other), h)
    far = ((c + 8) % 16, h)

    pending = []

    def remote(src, dst, sem, device, like=None):
        number = len(pending)
        pltpu.make_async_remote_copy(
            src_ref=src, dst_ref=dst, send_sem=send_sem.at[number], recv_sem=sem,
            device_id=device, device_id_type=MESH,
        ).start()
        pending.append(like or (lambda: src))

    def arrived(ref, sem):
        pltpu.make_async_remote_copy(
            src_ref=ref, dst_ref=ref, send_sem=send_sem.at[0], recv_sem=sem,
            device_id=sib, device_id_type=MESH,
        ).wait_recv()

    settled = []

    def settle(end):
        for number in range(len(settled), end):
            ref = pending[number]()
            pltpu.make_async_remote_copy(
                src_ref=ref, dst_ref=ref, send_sem=send_sem.at[number], recv_sem=one_sem.at[0],
                device_id=sib, device_id_type=MESH,
            ).wait_send()
            settled.append(number)

    def local(i, src, dst):
        copy = pltpu.make_async_copy(src, dst, local_sem.at[i])
        copy.start()
        return copy

    def cached(row, half, core, k):
        return kvc.at[row, half, :, pl.ds(pl.multiple_of(core * CACHE + k * CHUNK, 128), CHUNK)]

    own = pl.ds(pl.multiple_of(pp * CACHE, 128), CACHE)
    x_in = local(0, x_hbm, xbuf.at[h])
    k_in = local(1, ck_hbm, kvc.at[yy, bit, 0:HALF, own])
    v_in = local(2, cv_hbm, kvc.at[yy, bit, HALF:HEAD, own])
    wk_in = local(3, wk_hbm, wkv.at[0:HALF, :])
    wv_in = local(4, wv_hbm, wkv.at[HALF:HEAD, :])
    wq_in = [
        local(5 + i, wq_hbm.at[2048 * i : 2048 * (i + 1), :], wq.at[2048 * i : 2048 * (i + 1), :])
        for i in range(4)
    ]

    barrier = pltpu.get_barrier_semaphore()
    for device in (zp, zm, xp, yp, ym, sib, far):
        pl.semaphore_signal(barrier, inc=1, device_id=device, device_id_type=MESH)

    position = pos_ref[...]
    row_index = lax.broadcasted_iota(jnp.int32, (16, ROWS), 0)
    coarse = jnp.broadcast_to((position // 256).astype(jnp.float32), (16, ROWS))
    fine = jnp.broadcast_to((position % 256).astype(jnp.float32), (16, ROWS))
    places[0] = jnp.where(row_index == 0, coarse, jnp.where(row_index == 1, fine, 0.0)).astype(jnp.bfloat16)
    kvn[yy * 2 + pp, 2 * HEAD :, :] = places[0]
    pl.semaphore_wait(barrier, 7)

    def piece(kind, slot):
        return xbuf.at[slot, :, CUTS[kind][0] : CUTS[kind][1]]

    def send_x(kind, slot, device):
        remote(piece(kind, slot), piece(kind, slot), x_sem.at[kind, slot], device)

    def wait_x(kind, slot):
        arrived(piece(kind, slot), x_sem.at[kind, slot])

    def send_kv(row, half, core, k, device):
        block = cached(row, half, core, k)
        remote(block, block, kv_sem.at[row, half, core * CHUNKS + k], device, lambda: kvc.at[0, 0, :, 0:CHUNK])

    def wait_kv(row, half, core, k):
        arrived(cached(row, half, core, k), kv_sem.at[row, half, core * CHUNKS + k])

    def wait_row(row):
        for half in (0, 1):
            for k in range(CHUNKS):
                wait_kv(row, half, other, k)

    def send_new(row, core, device):
        slot = row * 2 + core
        remote(kvn.at[slot], kvn.at[slot], kvn_sem.at[slot], device, lambda: kvn.at[0])

    def wait_new(row, core):
        slot = row * 2 + core
        arrived(kvn.at[slot], kvn_sem.at[slot])

    across = head_at(1 - xl, z)

    def first_wave():
        x_in.wait()
        send_x(0, h, xp)
        for kind in (1, 0):
            send_x(kind, h, zp)
            send_x(kind, h, zm)
        send_x(1, h, xp)

    def second_wave():
        send_x(2, h, zp)
        send_x(2, h, zm)
        send_x(2, h, xp)
        wait_x(0, across)
        send_x(0, across, zp)
        send_x(0, across, zm)

    def ring(t, kind, col):
        for sign, ahead in ((1, zp), (-1, zm)):
            last = REACH[kind, sign]
            if t > last:
                continue
            slot = head_at(col, z - sign * t)
            wait_x(kind, slot)
            if t < last:
                send_x(kind, slot, ahead)
            if kind > 0:
                send_x(kind, slot, xp)

    def ring_step(t):
        ring(t, 1, xl)
        ring(t, 0, xl)
        ring(t, 2, xl)
        ring(t, 0, 1 - xl)

    def project(slot):
        block = xbuf[slot]
        start = pl.multiple_of(slot * COLS, COLS)
        q_sum[...] += jnp.dot(block, wq[pl.ds(start, COLS), :], preferred_element_type=jnp.float32)
        kv_sum[...] += lax.dot_general(
            wkv[:, pl.ds(start, COLS)], block, NT, preferred_element_type=jnp.float32
        )

    def steps(t):
        return (0,) if t == 0 else ((4,) if t == 4 else (t, -t))

    def own_column(t):
        for step in steps(t):
            project(head_at(xl, z - step))

    def other_column(t):
        for step in steps(t):
            slot = head_at(1 - xl, z - step)
            wait_x(1, slot)
            wait_x(2, slot)
            project(slot)

    def kv_start():
        k_in.wait()
        v_in.wait()
        for k in range(CHUNKS):
            for device in (yp, ym, sib):
                send_kv(yy, bit, pp, k, device)

    def kv_pair(k):
        send_kv(yy, bit, pp, k, pair)

    def kv_own_halves(k):
        wait_kv(yy, away, pp, k)
        for device in (yp, ym, sib):
            send_kv(yy, away, pp, k, device)

    def kv_forward(half, k):
        step = 2 * half - 1
        wait_kv(line(step), half, pp, k)
        send_kv(line(step), half, pp, k, (ctx_at(yy - step, pp), h))
        send_kv(line(step), half, pp, k, sib)

    def kv_rest(half, k):
        step = 1 - 2 * half
        wait_kv(line(step), half, pp, k)
        send_kv(line(step), half, pp, k, sib)

    def kv_opposite(half, k):
        wait_kv(line(2), half, pp, k)
        send_kv(line(2), half, pp, k, sib)

    def tables():
        angles = turn_ref[...] * position.astype(jnp.float32)
        cosine, sine = jnp.cos(angles), jnp.sin(angles)
        cos_k[...] = cosine
        sin_k[...] = sine
        cos_q[...] = jnp.concatenate([cosine, cosine], axis=0).T
        sin_q[...] = jnp.concatenate([-sine, sine], axis=0).T
        query_pos[0] = jnp.broadcast_to(position.astype(jnp.float32), (ROWS, ROWS)).T
        q_sum[...] = jnp.zeros_like(q_sum)
        kv_sum[...] = jnp.zeros_like(kv_sum)
        top[...] = jnp.full_like(top, NEGATIVE)
        total[...] = jnp.zeros_like(total)
        acc[...] = jnp.zeros_like(acc)

    first_wave()
    kv_start()
    remote(places.at[0], places.at[1], one_sem.at[0], far)
    second_wave()
    kv_pair(0)
    first = len(pending)
    tables()
    ring_step(1)
    second = len(pending)
    kv_pair(1)
    wk_in.wait()
    wv_in.wait()
    for copy in wq_in:
        copy.wait()
    own_column(0)
    ring_step(2)
    kv_pair(2)
    kv_own_halves(0)
    other_column(0)
    own_column(1)
    settle(first)
    ring_step(3)
    for k in range(CHUNKS):
        kv_forward(bit, k)
    for k in range(CHUNKS):
        kv_rest(bit, k)
    kv_own_halves(1)
    other_column(1)
    own_column(2)
    settle(second)
    ring_step(4)
    kv_own_halves(2)
    other_column(2)
    own_column(3)
    own_column(4)
    kv_forward(away, 0)
    other_column(3)
    other_column(4)

    raw[bit] = kv_sum[...].astype(jnp.bfloat16)
    remote(raw.at[bit], raw.at[bit], one_sem.at[1], pair)
    cosine, sine = cos_q[...], sin_q[...]
    scale = HEAD**-0.5 * LOG2E
    for j in range(4):
        part = q_sum[:, HEAD * j : HEAD * (j + 1)]
        turned = part * cosine + pltpu.roll(part, HALF, 1) * sine
        qs[0, ROWS * j : ROWS * (j + 1), :] = (turned * scale).astype(jnp.bfloat16)
    remote(qs.at[0], qs.at[1], one_sem.at[2], far)

    def new_rows():
        arrived(raw.at[away], one_sem.at[1])
        low, high = raw[0, 0:HALF, :].astype(jnp.float32), raw[1, 0:HALF, :].astype(jnp.float32)
        cosine, sine = cos_k[...], sin_k[...]
        slot = yy * 2 + pp
        kvn[slot, 0:HALF, :] = (low * cosine - high * sine).astype(jnp.bfloat16)
        kvn[slot, HALF:HEAD, :] = (high * cosine + low * sine).astype(jnp.bfloat16)
        kvn[slot, HEAD : HEAD + HALF, :] = raw[0, HALF:HEAD, :]
        kvn[slot, HEAD + HALF : 2 * HEAD, :] = raw[1, HALF:HEAD, :]
        for device in (yp, ym, sib):
            send_new(yy, pp, device)

    def new_from_sides():
        wait_new(line(-1), pp)
        send_new(line(-1), pp, yp)
        send_new(line(-1), pp, sib)
        wait_new(line(1), pp)
        send_new(line(1), pp, sib)

    def new_opposite():
        wait_new(line(2), pp)
        send_new(line(2), pp, sib)

    def soften(which, r, tiles, values):
        rows = slice(PART * r, PART * (r + 1))
        before = top[which, rows]
        highest = tiles[0]
        for tile in tiles[1:]:
            highest = jnp.maximum(highest, tile)
        now = jnp.maximum(before, jnp.max(highest, axis=1, keepdims=True))
        factor = jnp.exp2(before - now)
        weights = [jnp.exp2(tile - now) for tile in tiles]
        added = weights[0]
        for weight in weights[1:]:
            added = added + weight
        total[which, rows] = total[which, rows] * factor + added
        top[which, rows] = now
        packed = jnp.concatenate([weight.astype(jnp.bfloat16) for weight in weights], axis=1)
        acc[which, rows] = acc[which, rows] * factor + lax.dot_general(
            packed, values, NT, preferred_element_type=jnp.float32
        )

    def split(scores):
        return [scores[:, 128 * j : 128 * (j + 1)] for j in range(scores.shape[1] // 128)]

    def scores(which, row, r):
        keys = jnp.concatenate([kvc[row, 0, 0:HALF, :], kvc[row, 1, 0:HALF, :]], axis=0)
        return jnp.dot(qs[which, PART * r : PART * (r + 1), :], keys, preferred_element_type=jnp.float32)

    def cached_values(row):
        return jnp.concatenate([kvc[row, 0, HALF:HEAD, :], kvc[row, 1, HALF:HEAD, :]], axis=0)

    def job(i):
        which = (i + 3) // 4 % 2
        turn = (i + 3) % 4 * which + i // 5
        step = turn * (1 - turn // 2) + turn // 2 * (5 - turn)
        return which, line(step)

    def new_scores(which, r):
        keys = jnp.concatenate([kvn[s, 0:HEAD, :] for s in range(2 * LINES)], axis=1)
        return jnp.dot(qs[which, PART * r : PART * (r + 1), :], keys, preferred_element_type=jnp.float32)

    def soften_new(which, r, found):
        asked = jnp.concatenate([query_pos[which]] * (PART // ROWS), axis=0)
        tiles = []
        for s, tile in enumerate(split(found)):
            code = kvn[s, 2 * HEAD :, :].astype(jnp.float32)
            tiles.append(jnp.where(code[0:1] * 256.0 + code[1:2] <= asked, tile, NEGATIVE))
        values = jnp.concatenate([kvn[s, HEAD : 2 * HEAD, :] for s in range(2 * LINES)], axis=1)
        soften(which, r, tiles, values)

    for k in range(CHUNKS):
        kv_opposite(bit, k)
    wait_row(yy)
    sbuf[0] = scores(0, yy, 0)

    @pl.loop(0, 5)
    def _(i):
        @pl.when(i == 0)
        def _():
            new_rows()
            kv_forward(away, 1)
            kv_forward(away, 2)
            kv_rest(away, 0)
            kv_rest(away, 1)
            arrived(qs.at[1], one_sem.at[2])

        @pl.when(i == 1)
        def _():
            kv_rest(away, 2)
            wait_row(line(1))
            new_from_sides()

        @pl.when(i == 2)
        def _():
            for k in range(CHUNKS):
                kv_opposite(away, k)
            wait_row(line(3))

        @pl.when(i == 3)
        def _():
            new_opposite()
            wait_row(line(2))

        which, row = job(i)
        found = sbuf[0]
        sbuf[1] = scores(which, row, 1)
        values = cached_values(row)
        soften(which, 0, split(found), values)
        found = sbuf[1]
        next_which, next_row = job(i + 1)
        sbuf[0] = scores(next_which, next_row, 0)
        soften(which, 1, split(found), values)

    arrived(places.at[1], one_sem.at[0])
    code = places[1].astype(jnp.float32)
    query_pos[1] = jnp.broadcast_to(code[0:1] * 256.0 + code[1:2], (ROWS, ROWS)).T
    for step in range(LINES):
        wait_new(line(step), other)
    nbuf[0] = new_scores(1, 0)
    nbuf[1] = new_scores(1, 1)
    soften_new(1, 0, nbuf[0])
    soften_new(1, 1, nbuf[1])
    o_out[...] = acc[1].astype(jnp.bfloat16)
    lane = lax.broadcasted_iota(jnp.int32, (ROWS, HEAD), 1)
    state = jnp.zeros((ROWS, HEAD), jnp.float32)
    for j in range(4):
        rows = slice(ROWS * j, ROWS * (j + 1))
        state = jnp.where(lane == j, top[1, rows, :], state)
        state = jnp.where(lane == 4 + j, jnp.sum(total[1, rows, :], axis=1, keepdims=True), state)
    st_out[...] = state
    remote(st_out, st_in, one_sem.at[3], far)
    remote(o_out, o_in, one_sem.at[4], far)

    nbuf[0] = new_scores(0, 0)
    nbuf[1] = new_scores(0, 1)
    for i, step in ((5, 1), (6, 3), (7, 2)):
        which, row = 0, line(step)
        found = sbuf[0]
        sbuf[1] = scores(which, row, 1)
        values = cached_values(row)
        soften(which, 0, split(found), values)
        found = sbuf[1]
        if i < 7:
            sbuf[0] = scores(0, line(4 - step if step == 1 else 2), 0)
        soften(which, 1, split(found), values)
    soften_new(0, 0, nbuf[0])
    soften_new(0, 1, nbuf[1])

    settle(len(pending) - 2)
    arrived(st_in, one_sem.at[3])
    arrived(o_in, one_sem.at[4])
    state = st_in[...]
    for j in range(4):
        rows = slice(ROWS * j, ROWS * (j + 1))
        here, there = top[0, rows, :], state[:, j : j + 1]
        both = jnp.maximum(here, there)
        near_part, far_part = jnp.exp2(here - both), jnp.exp2(there - both)
        near_sum = jnp.sum(total[0, rows, :], axis=1, keepdims=True)
        weight_sum = near_sum * near_part + state[:, 4 + j : 5 + j] * far_part
        mixed = acc[0, rows, :] * near_part + o_in[rows, :].astype(jnp.float32) * far_part
        out_ref[:, HEAD * j : HEAD * (j + 1)] = (mixed / weight_sum).astype(jnp.bfloat16)

    settle(len(pending))


def per_device(
    new_states, query_weight, key_weight, value_weight, cache_keys, cache_values, new_positions
):
    turn = THETA ** (np.arange(HALF) * (-2.0 / HEAD))
    turn = jnp.asarray(np.repeat(turn[:, None], ROWS, axis=1), jnp.float32)
    hbm = pl.BlockSpec(memory_space=pl.ANY)
    vmem = pl.BlockSpec(memory_space=pltpu.VMEM)
    dma = pltpu.SemaphoreType.DMA
    bf16, f32 = jnp.bfloat16, jnp.float32
    scratch = [
        ((16, ROWS, COLS), bf16),
        ((8192, COLS), bf16),
        ((HEAD, 8192), bf16),
        ((LINES, 2, HEAD, 2 * CACHE), bf16),
        ((2 * LINES, 2 * HEAD + 16, ROWS), bf16),
        ((2, HEAD, ROWS), bf16),
        ((2, QROWS, HEAD), bf16),
        ((2, 16, ROWS), bf16),
        ((ROWS, COLS), f32),
        ((HEAD, ROWS), f32),
        ((2, QROWS, HEAD), f32),
        ((2, QROWS, HEAD), f32),
        ((2, QROWS, HEAD), f32),
        ((2, PART, 2 * CACHE), f32),
        ((2, PART, 2 * LINES * ROWS), f32),
        ((ROWS, HEAD), f32),
        ((ROWS, HEAD), f32),
        ((HALF, ROWS), f32),
        ((HALF, ROWS), f32),
        ((2, ROWS, HEAD), f32),
        ((QROWS, HEAD), bf16),
        ((QROWS, HEAD), bf16),
        ((ROWS, HEAD), f32),
        ((ROWS, HEAD), f32),
    ]
    return pl.pallas_call(
        kernel,
        out_shape=jax.ShapeDtypeStruct((ROWS, COLS), bf16),
        in_specs=[hbm] * 6 + [vmem] * 2,
        out_specs=vmem,
        scratch_shapes=[pltpu.VMEM(shape, kind) for shape, kind in scratch]
        + [dma((9,)), dma((3, 16)), dma((LINES, 2, 2 * CHUNKS)), dma((2 * LINES,)), dma((5,)), dma((SENDS,))],
        compiler_params=pltpu.CompilerParams(
            collective_id=0, has_side_effects=True, vmem_limit_bytes=56 << 20
        ),
    )(
        new_states, query_weight, key_weight.T, value_weight.T, cache_keys.T, cache_values.T,
        new_positions.reshape(1, ROWS), turn,
    )


def solution(mesh):
    placed = (
        P("ctx", "head"),
        P(None, "head"),
        P(None, "head"),
        P(None, "head"),
        P("ctx", "head"),
        P("ctx", "head"),
        P("ctx"),
    )
    return jax.shard_map(
        per_device, mesh=mesh, in_specs=placed, out_specs=P("ctx", "head"), check_vma=False
    )
```
